128 devices in a mesh: bead: 32 (over x, y, z_lo), space: 4 (over z_hi, core).
Axes of the slice: x: 4, y: 4, z: 4 (z_hi: 2, z_lo: 2; z = z_hi * 2 + z_lo), core: 2. Of those that a mesh axis runs over, the one named last changes fastest.
Arguments:
- positions: float32 [32, 3, 32768], P('bead', None, 'space'), may hold values from -6 to 6
- momenta: float32 [32, 3, 32768], P('bead', None, 'space'), may hold values from -6 to 6
- forces: float32 [32, 3, 32768], P('bead', None, 'space'), may hold values from -6 to 6
- gle_drift: float32 [32, 5, 5], replicated, may hold values from -0.25 to 0.98, as said below
- gle_noise_mix: float32 [32, 5, 5], replicated, may hold values from -1.5 to 1.5
- aux_momenta: float32 [32, 4, 3, 32768], P(None, None, None, ('space', 'bead')), may hold values from -6 to 6
- noise: float32 [2, 32, 5, 3, 32768], P(None, None, None, None, ('space', 'bead')), may hold values from -6 to 6
Outputs:
- positions_out: float32 [32, 3, 32768], P('bead', None, 'space')
- momenta_out: float32 [32, 3, 32768], P('bead', None, 'space')
- forces_out: float32 [32, 3, 32768], P('bead', None, 'space')
- aux_out: float32 [32, 4, 3, 32768], P(None, None, None, ('space', 'bead'))
The draws below stay inside these ranges and needn't reach their ends.
Inputs may be any that keep to these rules, and one draw needn't show every extreme that they name: `gle_drift`: one matrix a mode; diagonal entries positive.
All inputs are finite; a program needn't handle non-finite values.
Results may differ from the reference program's by a relative error of at most 0.00012.
Values sent between devices are 32-bit elements; how exact they have to be, the bound alone decides.
A program may use at most 64 MiB of HBM per device.

```python
import jax
import jax.numpy as jnp
from jax import lax

BEADS = 32
CELL_ATOMS = 128
AUX_MOMENTA = 4
STEPS = 2
DOMAIN_ATOMS = 8192
ATOMS = 32768
CELLS = 256
N_BEAD = 32
N_SPACE = 4


def draw_gle_drift(key, part):
    first, second = jax.random.split(jax.random.fold_in(key, 11))
    diagonal = jax.random.uniform(first, (BEADS, AUX_MOMENTA + 1), jnp.float32, 0.5, 0.95)
    outside = jax.random.uniform(second, (BEADS, AUX_MOMENTA + 1, AUX_MOMENTA + 1), jnp.float32, -0.25, 0.25)
    identity = jnp.eye(AUX_MOMENTA + 1, dtype=jnp.float32)[None]
    return outside * (1.0 - identity) + identity * diagonal[:, :, None]


def block_levels(own_key, dims, shards, least, top_value):
    loudness, own = 1.0, jax.random.fold_in(own_key, 6)
    for dim, shards_of in shards:
        draws = jnp.exp(jax.random.uniform(jax.random.fold_in(own, dim), (shards_of,), jnp.float32, least / len(shards), top_value / len(shards)))
        loudness = loudness * jnp.repeat(draws, dims[dim] // shards_of).reshape([-1 if axis == dim else 1 for axis in range(len(dims))])
    return loudness


def scatter_about(stream_key, shape, width, most, cuts=(), held_as=jnp.bfloat16):
    factor_of = block_levels(stream_key, shape, cuts, -0.22, 0.18) if cuts else 1.0
    values = jax.random.normal(stream_key, shape, jnp.float32) * width * factor_of
    return jnp.minimum(jnp.maximum(values, -most), most).astype(held_as)


def setup_inputs(seed: int = 0) -> dict:
    splits = jax.random.split(jax.random.key(seed), 8)
    positions = scatter_about(splits[0], (BEADS, 3, ATOMS), 1.0, 6.0, ((0, 32), (2, 4)), jnp.float32)
    momenta = scatter_about(splits[1], (BEADS, 3, ATOMS), 1.0, 6.0, ((0, 32), (2, 4)), jnp.float32)
    forces = scatter_about(splits[2], (BEADS, 3, ATOMS), 1.0, 6.0, ((0, 32), (2, 4)), jnp.float32)
    gle_drift = draw_gle_drift(jax.random.fold_in(splits[7], 71), 0)
    gle_noise_mix = scatter_about(splits[4], (BEADS, AUX_MOMENTA + 1, AUX_MOMENTA + 1), 0.3, 1.5, (), jnp.float32)
    aux_momenta = scatter_about(splits[5], (BEADS, AUX_MOMENTA, 3, ATOMS), 1.0, 6.0, ((3, 128),), jnp.float32)
    noise = scatter_about(splits[6], (STEPS, BEADS, AUX_MOMENTA + 1, 3, ATOMS), 1.0, 6.0, ((4, 128),), jnp.float32)
    return dict(positions=positions, momenta=momenta, forces=forces, gle_drift=gle_drift, gle_noise_mix=gle_noise_mix, aux_momenta=aux_momenta, noise=noise)


time_step = 0.5
cycle_freq = 1.5
cell_length = 2.0
pair_strength = 0.1
pair_range = 1.0

def mode_basis():
    index = jnp.arange(BEADS)
    bead_pos = index.astype(jnp.float32)[:, None]
    mode_pos = index.astype(jnp.float32)[None, :]
    phase = 2.0 * jnp.pi * bead_pos * mode_pos / BEADS
    kk = index[None, :]
    low = jnp.sqrt(1.0 / BEADS) + 0.0 * phase
    basis = jnp.where(kk == 0, low, jnp.where(kk < BEADS // 2, jnp.sqrt(2.0 / BEADS) * jnp.cos(phase), jnp.where(kk == BEADS // 2, jnp.sqrt(1.0 / BEADS) * jnp.cos(phase), jnp.sqrt(2.0 / BEADS) * jnp.sin(phase))))
    freq = 2.0 * cycle_freq * jnp.sin(jnp.pi * index.astype(jnp.float32) / BEADS)
    return (basis, freq, index)

def pull(center, other):
    sa = lax.optimization_barrier(jnp.sum(center * center, axis=0))
    sb = lax.optimization_barrier(jnp.sum(other * other, axis=0))
    cross = jnp.einsum('cni,cnj->nij', center, other, precision=lax.Precision.HIGHEST)
    dist = sa[:, :, None] + sb[:, None, :] - 2.0 * cross
    weight = jnp.exp(-dist / (2.0 * pair_range))
    rowsum = lax.optimization_barrier(jnp.sum(weight, axis=2))
    pulled = jnp.einsum('nij,cnj->cni', weight, other, precision=lax.Precision.HIGHEST)
    return pair_strength / pair_range * (center * rowsum[None] - pulled)

def bead_force(coords):
    cells = coords.reshape(3, CELLS, CELL_ATOMS)
    total = jnp.zeros_like(cells)
    for delta in (-1, 0, 1):
        other = jnp.roll(cells, -delta, axis=1)
        offset = jnp.asarray([delta * cell_length, 0.0, 0.0], dtype=cells.dtype).reshape(3, 1, 1)
        total = total + pull(cells, other + offset)
    return total.reshape(3, ATOMS)

def to_physical(values):
    lead = values.shape[:-1]
    share = DOMAIN_ATOMS // (2 * N_BEAD)
    grid = values.reshape(lead + (N_SPACE, N_BEAD, 2, share))
    return jnp.swapaxes(grid, -3, -2).reshape(lead + (ATOMS,))

def to_owner(values):
    lead = values.shape[:-1]
    share = DOMAIN_ATOMS // (2 * N_BEAD)
    grid = values.reshape(lead + (N_SPACE, 2, N_BEAD, share))
    return jnp.swapaxes(grid, -3, -2).reshape(lead + (ATOMS,))

def reference(positions, momenta, forces, gle_drift, gle_noise_mix, aux_momenta, noise):
    basis, freq, index = mode_basis()
    half = 0.5 * time_step
    aux = to_physical(aux_momenta)
    noise_phys = to_physical(noise)
    force = forces
    cosine = jnp.cos(time_step * freq)[:, None, None]
    safe = jnp.where(index == 0, 1.0, freq)
    sinc = jnp.where(index == 0, time_step, jnp.sin(time_step * freq) / safe)[:, None, None]
    wsin = (freq * jnp.sin(time_step * freq))[:, None, None]
    for step in range(STEPS):
        momenta = momenta + half * force
        qmode = jnp.einsum('jk,jcn->kcn', basis, positions, precision=lax.Precision.HIGHEST)
        pmode = jnp.einsum('jk,jcn->kcn', basis, momenta, precision=lax.Precision.HIGHEST)
        state = jnp.concatenate([pmode[:, None], aux], axis=1)
        state = jnp.einsum('kab,kbcn->kacn', gle_drift, state, precision=lax.Precision.HIGHEST) + jnp.einsum('kab,kbcn->kacn', gle_noise_mix, noise_phys[step], precision=lax.Precision.HIGHEST)
        pmode = state[:, 0]
        aux = state[:, 1:]
        qnext = qmode * cosine + sinc * pmode
        pmode = pmode * cosine - wsin * qmode
        positions = jnp.einsum('jk,kcn->jcn', basis, qnext, precision=lax.Precision.HIGHEST)
        momenta = jnp.einsum('jk,kcn->jcn', basis, pmode, precision=lax.Precision.HIGHEST)
        force = lax.map(bead_force, positions)
        momenta = momenta + half * force
    return (positions, momenta, force, to_owner(aux))
```

```python
import math

import jax
import jax.numpy as jnp
import numpy as np
from jax import lax
from jax.experimental import pallas as pl
from jax.experimental.pallas import tpu as pltpu
from jax.sharding import PartitionSpec as P

BEADS, OWNERS, SPACES, CELL, AUX, STEPS = 32, 32, 4, 128, 4, 2
TIME_STEP, FREQ, LENGTH, STRENGTH = 0.5, 1.5, 2.0, 0.1
HALF = 0.5 * TIME_STEP
SCALE = math.sqrt(math.log2(math.e))
SHIFT = LENGTH * SCALE
F32, BF16 = jnp.float32, jnp.bfloat16
MESH = pl.DeviceIdType.MESH
HIGHEST = lax.Precision.HIGHEST
UNROLL = 16


def constants():
    j = np.arange(BEADS, dtype=np.float64)
    phase = 2.0 * np.pi * j[:, None] * j[None, :] / BEADS
    k = j[None, :]
    basis = np.where(k < BEADS // 2, np.sqrt(2.0 / BEADS) * np.cos(phase), np.sqrt(2.0 / BEADS) * np.sin(phase))
    basis = np.where(k == 0, np.sqrt(1.0 / BEADS), basis)
    basis = np.where(k == BEADS // 2, np.sqrt(1.0 / BEADS) * np.cos(np.pi * j[:, None]), basis)
    freq = 2.0 * FREQ * np.sin(np.pi * j / BEADS)
    safe = np.where(j == 0, 1.0, freq)
    sinc = np.where(j == 0, TIME_STEP, np.sin(TIME_STEP * freq) / safe)
    out = np.zeros((5, BEADS, CELL), np.float32)
    out[0, :, :BEADS] = basis.T
    out[1, :, :BEADS] = basis
    out[2] = np.cos(TIME_STEP * freq)[:, None]
    out[3] = sinc[:, None]
    out[4] = (freq * np.sin(TIME_STEP * freq))[:, None]
    return out


def split3(x):
    a = x.astype(BF16).astype(F32)
    r = x - a
    b = r.astype(BF16).astype(F32)
    return a, b, r - b


def rhs_of(y):
    a, b, c = split3(y)
    return jnp.concatenate([a, b, a, b, c, a], axis=0).astype(BF16)


def lhs_of(x):
    a, b, c = split3(x)
    return jnp.concatenate([a, a, b, b, a, c], axis=0).T.astype(BF16)


def cell_force(x, ys):
    rhs = [rhs_of(y) for y in ys]
    right = jnp.concatenate(rhs, axis=1)
    left = jnp.concatenate([r[:16] for r in rhs], axis=1)
    e = lax.dot_general(lhs_of(x), right, (((1,), (0,)), ((), ())), preferred_element_type=F32)
    w = jnp.exp2(e)
    hi = w.astype(BF16)
    lo = (w - hi.astype(F32)).astype(BF16)
    nt = (((1,), (1,)), ((), ()))
    o = lax.dot_general(left, hi, nt, preferred_element_type=F32)
    o = o + lax.dot_general(left, lo, nt, preferred_element_type=F32)
    s = o[:8] + o[8:]
    return (STRENGTH / SCALE) * (x * s[3:4] - s)


def put_points(ref, base, tiles, shift, center):
    n = tiles[0].shape[0]
    t = [tiles[0] + shift, tiles[1], tiles[2]] if shift else list(tiles)
    norm = -0.5 * (t[0] * t[0] + t[1] * t[1] + t[2] * t[2])
    one = jnp.ones_like(norm)
    t += [norm, one] if center else [one, norm]
    t += [jnp.zeros_like(norm)] * 3
    for r, v in enumerate(t):
        ref[pl.ds(base + r, n, stride=8), :] = v


def all_forces(px, pm, p0, pp, fb, after):
    def step(i, carry):
        for u in range(UNROLL):
            at = pl.multiple_of((i * UNROLL + u) * 8, 8)
            nxt = pl.multiple_of(at + after, 8)
            ys = [pm[pl.ds(at, 8), :], p0[pl.ds(at, 8), :], pp[pl.ds(nxt, 8), :]]
            fb[pl.ds(at, 8), :] = cell_force(px[pl.ds(at, 8), :], ys)
        return carry

    lax.fori_loop(0, 64 // UNROLL, step, 0)


TILES = [(c, h) for c in range(3) for h in range(2)]


def mm(a, b):
    return jnp.dot(a, b, precision=HIGHEST, preferred_element_type=F32)


def exchange(me, send, recv, ssem, rsem):
    def copy(peer, slot):
        return pltpu.make_async_remote_copy(
            src_ref=send.at[pl.ds(pl.multiple_of(peer * 16, 16), 16)],
            dst_ref=recv.at[pl.ds(pl.multiple_of(slot * 16, 16), 16)],
            send_sem=ssem.at[peer],
            recv_sem=rsem.at[slot],
            device_id={"bead": peer},
            device_id_type=MESH,
        )

    def start(k, carry):
        copy(lax.rem(me + k, OWNERS), me).start()
        return carry

    lax.fori_loop(1, OWNERS, start, 0)
    own = pl.ds(pl.multiple_of(me * 16, 16), 16)
    recv[own, :] = send[own, :]

    def arrive(k, carry):
        peer = lax.rem(me + OWNERS - k, OWNERS)
        copy(peer, peer).wait_recv()
        return carry

    def sent(k, carry):
        copy(lax.rem(me + k, OWNERS), me).wait_send()
        return carry

    return (
        lambda: lax.fori_loop(1, OWNERS, arrive, 0),
        lambda: lax.fori_loop(1, OWNERS, sent, 0),
    )


def body(
    q_hbm, p_hbm, f_hbm, dr_hbm, mx_hbm, aux_hbm, noise_hbm, cst_hbm,
    q_out, p_out, f_out, aux_out,
    q, p, f, dr, mx, aux, noise, cst,
    send, recv, send2, recv2, edge, coef, u, u2, hs, hr,
    px, pm, p0, pp, fb,
    lsem, s1, r1, s2, r2, hssem, hrsem, essem, ersem,
):
    s, me = lax.axis_index("space"), lax.axis_index("bead")
    loads = [
        pltpu.make_async_copy(a, b, lsem.at[i])
        for i, (a, b) in enumerate(
            [(q_hbm, q), (p_hbm, p), (f_hbm, f), (dr_hbm, dr), (mx_hbm, mx), (aux_hbm, aux), (noise_hbm, noise), (cst_hbm, cst)]
        )
    ]
    for c in loads:
        c.start()
    barrier = pltpu.get_barrier_semaphore()
    up, down = lax.rem(s + 1, SPACES), lax.rem(s + SPACES - 1, SPACES)

    def greet(k, carry):
        pl.semaphore_signal(barrier, inc=1, device_id={"bead": lax.rem(me + k, OWNERS)}, device_id_type=MESH)
        return carry

    lax.fori_loop(1, OWNERS, greet, 0)
    for side in (up, down):
        pl.semaphore_signal(barrier, inc=1, device_id={"space": side}, device_id_type=MESH)
        pl.semaphore_signal(barrier, inc=1, device_id={"space": side, "bead": OWNERS - 1 - me}, device_id_type=MESH)

    for c in loads[:3]:
        c.wait()
    for h in range(2):
        for c in range(3):
            rows = pl.ds(h * 32, 32)
            send[pl.ds(h * 4 + c, 32, stride=16), :] = q[c, rows, :]
            send[pl.ds(8 + h * 4 + c, 32, stride=16), :] = p[c, rows, :] + HALF * f[c, rows, :]
    pl.semaphore_wait(barrier, OWNERS - 1 + 4)
    arrived, sent = exchange(me, send, recv, s1, r1)

    for c in loads[3:]:
        c.wait()
    for m, ref in enumerate((dr, mx)):
        for a in range(5):
            cols = ref[a].T
            for b in range(5):
                coef[m, a, b] = jnp.broadcast_to(cols[:, b : b + 1], (BEADS, CELL))
    for t, (c, h) in enumerate(TILES):
        lanes = pl.ds(t * CELL, CELL)
        state = [aux[pl.ds(c * 8 + h * 4 + a, 32, stride=24), :] for a in range(AUX)]
        kick = [[noise[st, b, c, :, pl.ds(h * CELL, CELL)] for b in range(5)] for st in range(STEPS)]
        for a in range(5):
            total = coef[1, a, 0] * kick[0][0]
            later = coef[1, a, 0] * kick[1][0]
            for b in range(1, 5):
                total = total + coef[1, a, b] * kick[0][b]
                later = later + coef[1, a, b] * kick[1][b]
            for b in range(AUX):
                total = total + coef[0, a, b + 1] * state[b]
            u[a, :, lanes] = total
            u2[a, :, lanes] = later

    arrived()
    fwd, inv = cst[0][:, :BEADS], cst[1][:, :BEADS]
    wide = lambda v: jnp.concatenate([v] * 6, axis=1)
    cosine, sinc, wsin = wide(cst[2]), wide(cst[3]), wide(cst[4])
    drift0 = [wide(coef[0, a, 0]) for a in range(5)]

    def free(qm, pm_, kick):
        z = drift0[0] * pm_ + kick[0]
        rest = [drift0[a] * pm_ + kick[a] for a in range(1, 5)]
        return qm * cosine + sinc * z, z * cosine - wsin * qm, rest

    qm = mm(fwd, jnp.concatenate([recv[pl.ds(h * 4 + c, 32, stride=16), :] for c, h in TILES], axis=1))
    pmode = mm(fwd, jnp.concatenate([recv[pl.ds(8 + h * 4 + c, 32, stride=16), :] for c, h in TILES], axis=1))
    qm, pmode, state = free(qm, pmode, u)
    points = mm(inv, qm) * SCALE
    tile = lambda v, c, h: v[:, (2 * c + h) * CELL : (2 * c + h + 1) * CELL]
    for h in range(2):
        for c in range(3):
            hs[h, c] = tile(points, c, h)

    halo = []
    for h in range(2):
        mine = s * 64 + h * 32 + me
        for side, step in ((0, 1), (1, 255)):
            there = lax.rem(mine + step, 256)
            slot = lax.rem(there // 32, 2)
            halo.append(
                pltpu.make_async_remote_copy(
                    src_ref=hs.at[h],
                    dst_ref=hr.at[side, slot],
                    send_sem=hssem.at[side, h],
                    recv_sem=hrsem.at[side, slot],
                    device_id={"space": there // 64, "bead": lax.rem(there, 32)},
                    device_id_type=MESH,
                )
            )
    for c in halo:
        c.start()
    for h in range(2):
        mine = [tile(points, c, h) for c in range(3)]
        put_points(px, h * 256, mine, 0.0, True)
        put_points(p0, h * 256, mine, 0.0, False)
    for a in range(5):
        total = u2[a]
        for b in range(AUX):
            total = total + wide(coef[0, a, b + 1]) * state[b]
        u2[a] = total
    for side, (ref, shift) in enumerate(((pm, -SHIFT), (pp, SHIFT))):
        for h in range(2):
            pltpu.make_async_remote_copy(
                src_ref=hs.at[h], dst_ref=hr.at[side, h], send_sem=hssem.at[side, h], recv_sem=hrsem.at[side, h],
                device_id={"space": up}, device_id_type=MESH,
            ).wait_recv()
            put_points(ref, h * 256, [hr[side, h, c] for c in range(3)], shift, False)
    all_forces(px, pm, p0, pp, fb, 0)
    force = jnp.concatenate([fb[pl.ds(h * 256 + c, 32, stride=8), :] for c, h in TILES], axis=1)
    pmode = pmode + 2.0 * HALF * mm(fwd, force)
    qm, pmode, state = free(qm, pmode, u2)
    qb, pb = mm(inv, qm), mm(inv, pmode)
    for c, h in TILES:
        send2[pl.ds(h * 4 + c, 32, stride=16), :] = tile(qb, c, h)
        send2[pl.ds(8 + h * 4 + c, 32, stride=16), :] = tile(pb, c, h)
    arrived2, sent2 = exchange(me, send2, recv2, s2, r2)
    for c, h in TILES:
        for a in range(AUX):
            aux_out[pl.ds(c * 8 + h * 4 + a, 32, stride=24), :] = tile(state[a], c, h)
    for c in halo:
        c.wait_send()
    sent()
    arrived2()
    edges = [
        pltpu.make_async_remote_copy(
            src_ref=recv2.at[pl.ds(src * 16, 8)],
            dst_ref=edge.at[pl.ds(side * 8, 8)],
            send_sem=essem.at[side],
            recv_sem=ersem.at[side],
            device_id={"space": where},
            device_id_type=MESH,
        )
        for side, (src, where) in enumerate(((OWNERS - 1, up), (0, down)))
    ]
    for c in edges:
        c.start()
    for h in range(2):
        tiles = []
        for c in range(3):
            t = recv2[pl.ds(h * 4 + c, 32, stride=16), :]
            q_out[c, pl.ds(h * 32, 32), :] = t
            tiles.append(t * SCALE)
        put_points(px, h * 256, tiles, 0.0, True)
        put_points(p0, h * 256, tiles, 0.0, False)
        put_points(pm, h * 256 + 8, tiles, -SHIFT, False)
        put_points(pp, h * 256, tiles, SHIFT, False)
    for c in edges:
        c.wait_recv()
    put_points(pm, 0, [edge[4 + c : 5 + c, :] * SCALE for c in range(3)], -SHIFT, False)
    put_points(pp, 512, [edge[8 + c : 9 + c, :] * SCALE for c in range(3)], SHIFT, False)
    all_forces(px, pm, p0, pp, fb, 8)
    for h in range(2):
        rows = pl.ds(h * 32, 32)
        for c in range(3):
            force = fb[pl.ds(h * 256 + c, 32, stride=8), :]
            f_out[c, rows, :] = force
            p_out[c, rows, :] = recv2[pl.ds(8 + h * 4 + c, 32, stride=16), :] + HALF * force
    for c in edges:
        c.wait_send()
    sent2()


def on_device(positions, momenta, forces, gle_drift, gle_noise_mix, aux_momenta, noise):
    cells = lambda v: v.reshape(3, 64, CELL)
    modes_last = lambda v: jnp.transpose(v, (1, 2, 0))
    aux = jnp.transpose(aux_momenta.reshape(BEADS, AUX, 3, 2, CELL), (0, 2, 3, 1, 4)).reshape(768, CELL)
    kicks = jnp.transpose(noise, (0, 2, 3, 1, 4))
    big = jax.ShapeDtypeStruct((3, 64, CELL), F32)
    vm = lambda *shape: pltpu.VMEM(shape, F32)
    dma = lambda *shape: pltpu.SemaphoreType.DMA(shape)
    any_, vmem = pl.BlockSpec(memory_space=pl.ANY), pl.BlockSpec(memory_space=pltpu.VMEM)
    q, p, f, a = pl.pallas_call(
        body,
        out_shape=(big, big, big, jax.ShapeDtypeStruct((768, CELL), F32)),
        in_specs=[any_] * 8,
        out_specs=(vmem,) * 4,
        scratch_shapes=[
            vm(3, 64, CELL), vm(3, 64, CELL), vm(3, 64, CELL), vm(5, 5, BEADS), vm(5, 5, BEADS),
            vm(768, CELL), vm(2, 5, 3, BEADS, 256), vm(5, BEADS, CELL),
            vm(512, CELL), vm(512, CELL), vm(512, CELL), vm(512, CELL), vm(16, CELL),
            vm(2, 5, 5, BEADS, CELL), vm(5, BEADS, 768), vm(5, BEADS, 768),
            vm(2, 3, BEADS, CELL), vm(2, 2, 3, BEADS, CELL),
            *([vm(520, CELL)] * 5),
            dma(8), dma(OWNERS), dma(OWNERS), dma(OWNERS), dma(OWNERS), dma(2, 2), dma(2, 2), dma(2), dma(2),
        ],
        compiler_params=pltpu.CompilerParams(collective_id=0, has_side_effects=True),
    )(cells(positions), cells(momenta), cells(forces), modes_last(gle_drift), modes_last(gle_noise_mix), aux, kicks, jnp.asarray(constants()))
    aux_new = jnp.transpose(a.reshape(BEADS, 3, 2, AUX, CELL), (0, 3, 1, 2, 4)).reshape(BEADS, AUX, 3, 256)
    back = lambda v: v.reshape(1, 3, 8192)
    return back(q), back(p), back(f), aux_new


def solution(mesh):
    wide = P("bead", None, "space")
    aux = P(None, None, None, ("space", "bead"))
    noise = P(None, None, None, None, ("space", "bead"))
    return jax.shard_map(
        on_device, mesh=mesh, in_specs=(wide, wide, wide, P(), P(), aux, noise),
        out_specs=(wide, wide, wide, aux), check_vma=False,
    )
```

```python
import math

import jax
import jax.numpy as jnp
import numpy as np
from jax import lax
from jax.experimental import pallas as pl
from jax.experimental.pallas import tpu as pltpu
from jax.sharding import PartitionSpec as P

BEADS, OWNERS, SPACES, CELL, AUX, STEPS = 32, 32, 4, 128, 4, 2
TIME_STEP, FREQ, LENGTH, STRENGTH = 0.5, 1.5, 2.0, 0.1
HALF = 0.5 * TIME_STEP
SCALE = math.sqrt(math.log2(math.e))
SHIFT = LENGTH * SCALE
F32, BF16 = jnp.float32, jnp.bfloat16
MESH = pl.DeviceIdType.MESH
HIGHEST = lax.Precision.HIGHEST
AHEAD = 4


def constants():
    j = np.arange(BEADS, dtype=np.float64)
    phase = 2.0 * np.pi * j[:, None] * j[None, :] / BEADS
    k = j[None, :]
    basis = np.where(k < BEADS // 2, np.sqrt(2.0 / BEADS) * np.cos(phase), np.sqrt(2.0 / BEADS) * np.sin(phase))
    basis = np.where(k == 0, np.sqrt(1.0 / BEADS), basis)
    basis = np.where(k == BEADS // 2, np.sqrt(1.0 / BEADS) * np.cos(np.pi * j[:, None]), basis)
    freq = 2.0 * FREQ * np.sin(np.pi * j / BEADS)
    safe = np.where(j == 0, 1.0, freq)
    sinc = np.where(j == 0, TIME_STEP, np.sin(TIME_STEP * freq) / safe)
    out = np.zeros((5, BEADS, CELL), np.float32)
    out[0, :, :BEADS] = basis.T
    out[1, :, :BEADS] = basis
    out[2] = np.cos(TIME_STEP * freq)[:, None]
    out[3] = sinc[:, None]
    out[4] = (freq * np.sin(TIME_STEP * freq))[:, None]
    return out


def split3(x):
    a = x.astype(BF16).astype(F32)
    r = x - a
    b = r.astype(BF16).astype(F32)
    return a, b, r - b


def rhs_of(y):
    a, b, c = split3(y)
    return jnp.concatenate([a, b, a, b, c, a], axis=0).astype(BF16)


def lhs_of(x):
    a, b, c = split3(x)
    return jnp.concatenate([a, a, b, b, a, c], axis=0).T.astype(BF16)


def exponents(x, ys):
    rhs = [rhs_of(y) for y in ys]
    left = jnp.concatenate([r[:16] for r in rhs for _ in range(2)], axis=1)
    right = jnp.concatenate(rhs, axis=1)
    return lax.dot_general(lhs_of(x), right, (((1,), (0,)), ((), ())), preferred_element_type=F32), left


def pulls(e, left):
    parts = []
    for k in range(e.shape[1] // CELL):
        w = jnp.exp2(e[:, k * CELL : (k + 1) * CELL])
        hi = w.astype(BF16)
        parts += [hi, (w - hi.astype(F32)).astype(BF16)]
    w = jnp.concatenate(parts, axis=1)
    o = lax.dot_general(left, w, (((1,), (1,)), ((), ())), preferred_element_type=F32)
    return o[:8] + o[8:]


def pipelined(cells, first, second):
    todo = []
    for i in range(len(cells) + AHEAD):
        if i < len(cells):
            todo.append(first(cells[i]))
        if i >= AHEAD:
            second(cells[i - AHEAD], *todo[i - AHEAD])


def put_points(ref, base, tiles, shift, center):
    n = tiles[0].shape[0]
    t = [tiles[0] + shift, tiles[1], tiles[2]] if shift else list(tiles)
    norm = -0.5 * (t[0] * t[0] + t[1] * t[1] + t[2] * t[2])
    one = jnp.ones_like(norm)
    t += [norm, one] if center else [one, norm]
    t += [jnp.zeros_like(norm)] * 3
    for r, v in enumerate(t):
        ref[pl.ds(base + r, n, stride=8), :] = v


def at(c):
    return pl.ds(c * 8, 8)


def force_of(x, s):
    return (STRENGTH / SCALE) * (x * s[3:4] - s)


def own_cells(px, p0, fb):
    def second(c, e, left):
        fb[at(c), :] = pulls(e, left)

    pipelined(range(64), lambda c: exponents(px[at(c), :], [p0[at(c), :]]), second)


def next_cells(px, pm, pp, fb):
    def second(c, e, left):
        fb[at(c), :] = force_of(px[at(c), :], fb[at(c), :] + pulls(e, left))

    pipelined(range(64), lambda c: exponents(px[at(c), :], [pm[at(c), :], pp[at(c), :]]), second)


def three_cells(cells, px, pm, p0, pp, fb):
    def second(c, e, left):
        fb[at(c), :] = force_of(px[at(c), :], pulls(e, left))

    pipelined(cells, lambda c: exponents(px[at(c), :], [pm[at(c), :], p0[at(c), :], pp[at(c + 1), :]]), second)


TILES = [(c, h) for c in range(3) for h in range(2)]


def mm(a, b):
    return jnp.dot(a, b, precision=HIGHEST, preferred_element_type=F32)


def exchange(me, send, recv, ssem, rsem):
    def copy(peer, slot):
        return pltpu.make_async_remote_copy(
            src_ref=send.at[pl.ds(pl.multiple_of(peer * 16, 16), 16)],
            dst_ref=recv.at[pl.ds(pl.multiple_of(slot * 16, 16), 16)],
            send_sem=ssem.at[peer],
            recv_sem=rsem.at[slot],
            device_id={"bead": peer},
            device_id_type=MESH,
        )

    def start(k, carry):
        copy(lax.rem(me + k, OWNERS), me).start()
        return carry

    lax.fori_loop(1, OWNERS, start, 0)
    own = pl.ds(pl.multiple_of(me * 16, 16), 16)
    recv[own, :] = send[own, :]

    def wait(peer):
        @pl.when(peer != me)
        def _():
            copy(peer, peer).wait_recv()

    def arrive(peer, carry):
        wait(peer)
        return carry

    def sent(k, carry):
        copy(lax.rem(me + k, OWNERS), me).wait_send()
        return carry

    def ends():
        wait(OWNERS - 1)
        wait(0)

    return (
        ends,
        lambda: lax.fori_loop(1, OWNERS - 1, arrive, 0),
        lambda: lax.fori_loop(1, OWNERS, sent, 0),
    )


def body(
    q_hbm, p_hbm, f_hbm, dr_hbm, mx_hbm, aux_hbm, noise_hbm, cst_hbm,
    q_out, p_out, f_out, aux_out,
    q, p, f, dr, mx, aux, noise, cst,
    send, recv, send2, recv2, edge, coef, u, u2, hs, hr,
    px, pm, p0, pp, fb,
    lsem, s1, r1, s2, r2, hssem, hrsem, essem, ersem,
):
    s, me = lax.axis_index("space"), lax.axis_index("bead")
    loads = [
        pltpu.make_async_copy(a, b, lsem.at[i])
        for i, (a, b) in enumerate(
            [(q_hbm, q), (p_hbm, p), (f_hbm, f), (dr_hbm, dr), (mx_hbm, mx), (aux_hbm, aux), (noise_hbm, noise), (cst_hbm, cst)]
        )
    ]
    for c in loads:
        c.start()
    barrier = pltpu.get_barrier_semaphore()
    up, down = lax.rem(s + 1, SPACES), lax.rem(s + SPACES - 1, SPACES)

    def greet(k, carry):
        pl.semaphore_signal(barrier, inc=1, device_id={"bead": lax.rem(me + k, OWNERS)}, device_id_type=MESH)
        return carry

    lax.fori_loop(1, OWNERS, greet, 0)
    for side in (up, down):
        pl.semaphore_signal(barrier, inc=1, device_id={"space": side}, device_id_type=MESH)

    first, last = me == 0, me == OWNERS - 1

    @pl.when(jnp.logical_or(first, last))
    def _():
        there, bead = jnp.where(first, down, up), OWNERS - 1 - me
        pl.semaphore_signal(barrier, inc=1, device_id={"space": there, "bead": bead}, device_id_type=MESH)

    for c in loads[:3]:
        c.wait()
    for h in range(2):
        for c in range(3):
            rows = pl.ds(h * 32, 32)
            send[pl.ds(h * 4 + c, 32, stride=16), :] = q[c, rows, :]
            send[pl.ds(8 + h * 4 + c, 32, stride=16), :] = p[c, rows, :] + HALF * f[c, rows, :]
    pl.semaphore_wait(barrier, OWNERS - 1 + 2 + jnp.where(jnp.logical_or(first, last), 1, 0))
    ends, arrived, sent = exchange(me, send, recv, s1, r1)

    for c in loads[3:]:
        c.wait()
    for m, ref in enumerate((dr, mx)):
        for a in range(5):
            cols = ref[a].T
            for b in range(5):
                coef[m, a, b] = jnp.broadcast_to(cols[:, b : b + 1], (BEADS, CELL))
    for t, (c, h) in enumerate(TILES):
        lanes = pl.ds(t * CELL, CELL)
        state = [aux[pl.ds(c * 8 + h * 4 + a, 32, stride=24), :] for a in range(AUX)]
        kick = [[noise[st, b, c, :, pl.ds(h * CELL, CELL)] for b in range(5)] for st in range(STEPS)]
        for a in range(5):
            total = coef[1, a, 0] * kick[0][0]
            later = coef[1, a, 0] * kick[1][0]
            for b in range(1, 5):
                total = total + coef[1, a, b] * kick[0][b]
                later = later + coef[1, a, b] * kick[1][b]
            for b in range(AUX):
                total = total + coef[0, a, b + 1] * state[b]
            u[a, :, lanes] = total
            u2[a, :, lanes] = later

    ends()
    arrived()
    fwd, inv = cst[0][:, :BEADS], cst[1][:, :BEADS]
    wide = lambda v: jnp.concatenate([v] * 6, axis=1)
    cosine, sinc, wsin = wide(cst[2]), wide(cst[3]), wide(cst[4])
    drift0 = [wide(coef[0, a, 0]) for a in range(5)]

    def free(qm, pm_, kick):
        z = drift0[0] * pm_ + kick[0]
        rest = [drift0[a] * pm_ + kick[a] for a in range(1, 5)]
        return qm * cosine + sinc * z, z * cosine - wsin * qm, rest

    qm = mm(fwd, jnp.concatenate([recv[pl.ds(h * 4 + c, 32, stride=16), :] for c, h in TILES], axis=1))
    pmode = mm(fwd, jnp.concatenate([recv[pl.ds(8 + h * 4 + c, 32, stride=16), :] for c, h in TILES], axis=1))
    qm, pmode, state = free(qm, pmode, u)
    points = mm(inv, qm) * SCALE
    tile = lambda v, c, h: v[:, (2 * c + h) * CELL : (2 * c + h + 1) * CELL]
    for h in range(2):
        for c in range(3):
            hs[h, c] = tile(points, c, h)

    halo = []
    for h in range(2):
        mine = s * 64 + h * 32 + me
        for side, step in ((0, 1), (1, 255)):
            there = lax.rem(mine + step, 256)
            slot = lax.rem(there // 32, 2)
            halo.append(
                pltpu.make_async_remote_copy(
                    src_ref=hs.at[h],
                    dst_ref=hr.at[side, slot],
                    send_sem=hssem.at[side, h],
                    recv_sem=hrsem.at[side, slot],
                    device_id={"space": there // 64, "bead": lax.rem(there, 32)},
                    device_id_type=MESH,
                )
            )
    for c in halo:
        c.start()
    for h in range(2):
        mine = [tile(points, c, h) for c in range(3)]
        put_points(px, h * 256, mine, 0.0, True)
        put_points(p0, h * 256, mine, 0.0, False)
    for a in range(5):
        total = u2[a]
        for b in range(AUX):
            total = total + wide(coef[0, a, b + 1]) * state[b]
        u2[a] = total
    own_cells(px, p0, fb)
    for side, (ref, shift) in enumerate(((pm, -SHIFT), (pp, SHIFT))):
        for h in range(2):
            pltpu.make_async_remote_copy(
                src_ref=hs.at[h], dst_ref=hr.at[side, h], send_sem=hssem.at[side, h], recv_sem=hrsem.at[side, h],
                device_id={"space": up}, device_id_type=MESH,
            ).wait_recv()
            put_points(ref, h * 256, [hr[side, h, c] for c in range(3)], shift, False)
    next_cells(px, pm, pp, fb)
    force = jnp.concatenate([fb[pl.ds(h * 256 + c, 32, stride=8), :] for c, h in TILES], axis=1)
    pmode = pmode + 2.0 * HALF * mm(fwd, force)
    qm, pmode, state = free(qm, pmode, u2)
    qb, pb = mm(inv, qm), mm(inv, pmode)
    for c, h in TILES:
        send2[pl.ds(h * 4 + c, 32, stride=16), :] = tile(qb, c, h)
        send2[pl.ds(8 + h * 4 + c, 32, stride=16), :] = tile(pb, c, h)
    ends2, arrived2, sent2 = exchange(me, send2, recv2, s2, r2)
    for c, h in TILES:
        for a in range(AUX):
            aux_out[pl.ds(c * 8 + h * 4 + a, 32, stride=24), :] = tile(state[a], c, h)
    for c in halo:
        c.wait_send()
    sent()
    ends2()
    edges = [
        pltpu.make_async_remote_copy(
            src_ref=recv2.at[pl.ds(src * 16, 8)],
            dst_ref=edge.at[pl.ds(side * 8, 8)],
            send_sem=essem.at[side],
            recv_sem=ersem.at[side],
            device_id={"space": where},
            device_id_type=MESH,
        )
        for side, (src, where) in enumerate(((OWNERS - 1, up), (0, down)))
    ]
    for c in edges:
        c.start()
    arrived2()
    for h in range(2):
        tiles = []
        for c in range(3):
            t = recv2[pl.ds(h * 4 + c, 32, stride=16), :]
            q_out[c, pl.ds(h * 32, 32), :] = t
            tiles.append(t * SCALE)
        put_points(px, h * 256, tiles, 0.0, True)
        put_points(p0, h * 256, tiles, 0.0, False)
        put_points(pm, h * 256 + 8, tiles, -SHIFT, False)
        put_points(pp, h * 256, tiles, SHIFT, False)
    three_cells(range(1, 63), px, pm, p0, pp, fb)
    for c in edges:
        c.wait_recv()
    put_points(pm, 0, [edge[4 + c : 5 + c, :] * SCALE for c in range(3)], -SHIFT, False)
    put_points(pp, 512, [edge[8 + c : 9 + c, :] * SCALE for c in range(3)], SHIFT, False)
    three_cells((0, 63), px, pm, p0, pp, fb)
    for h in range(2):
        rows = pl.ds(h * 32, 32)
        for c in range(3):
            force = fb[pl.ds(h * 256 + c, 32, stride=8), :]
            f_out[c, rows, :] = force
            p_out[c, rows, :] = recv2[pl.ds(8 + h * 4 + c, 32, stride=16), :] + HALF * force
    for c in edges:
        c.wait_send()
    sent2()


def hand_over(*refs):
    copies = [pltpu.make_async_copy(refs[i], refs[4 + i], refs[8].at[i]) for i in range(4)]
    for c in copies:
        c.start()
    for c in copies:
        c.wait()


def on_device(positions, momenta, forces, gle_drift, gle_noise_mix, aux_momenta, noise):
    cells = lambda v: v.reshape(3, 64, CELL)
    modes_last = lambda v: jnp.transpose(v, (1, 2, 0))
    aux = jnp.transpose(aux_momenta.reshape(BEADS, AUX, 3, 2, CELL), (0, 2, 3, 1, 4)).reshape(768, CELL)
    kicks = jnp.transpose(noise, (0, 2, 3, 1, 4))
    big = jax.ShapeDtypeStruct((3, 64, CELL), F32)
    vm = lambda *shape: pltpu.VMEM(shape, F32)
    dma = lambda *shape: pltpu.SemaphoreType.DMA(shape)
    any_, vmem = pl.BlockSpec(memory_space=pl.ANY), pl.BlockSpec(memory_space=pltpu.VMEM)
    shapes = ((3, 64, CELL),) * 3 + ((768, CELL),)
    results = pl.pallas_call(
        body,
        out_shape=tuple(pltpu.VMEM(x, F32) for x in shapes),
        in_specs=[any_] * 8,
        out_specs=(vmem,) * 4,
        scratch_shapes=[
            vm(3, 64, CELL), vm(3, 64, CELL), vm(3, 64, CELL), vm(5, 5, BEADS), vm(5, 5, BEADS),
            vm(768, CELL), vm(2, 5, 3, BEADS, 256), vm(5, BEADS, CELL),
            vm(512, CELL), vm(512, CELL), vm(512, CELL), vm(512, CELL), vm(16, CELL),
            vm(2, 5, 5, BEADS, CELL), vm(5, BEADS, 768), vm(5, BEADS, 768),
            vm(2, 3, BEADS, CELL), vm(2, 2, 3, BEADS, CELL),
            *([vm(520, CELL)] * 5),
            dma(8), dma(OWNERS), dma(OWNERS), dma(OWNERS), dma(OWNERS), dma(2, 2), dma(2, 2), dma(2), dma(2),
        ],
        compiler_params=pltpu.CompilerParams(collective_id=0, has_side_effects=True),
    )(cells(positions), cells(momenta), cells(forces), modes_last(gle_drift), modes_last(gle_noise_mix), aux, kicks, jnp.asarray(constants()))
    q, p, f, a = pl.pallas_call(
        hand_over,
        out_shape=tuple(jax.ShapeDtypeStruct(x, F32) for x in shapes),
        in_specs=[any_] * 4,
        out_specs=(any_,) * 4,
        scratch_shapes=[dma(4)],
    )(*[pltpu.with_memory_space_constraint(x, pltpu.VMEM) for x in results])
    aux_new = jnp.transpose(a.reshape(BEADS, 3, 2, AUX, CELL), (0, 3, 1, 2, 4)).reshape(BEADS, AUX, 3, 256)
    back = lambda v: v.reshape(1, 3, 8192)
    return back(q), back(p), back(f), aux_new


def solution(mesh):
    wide = P("bead", None, "space")
    aux = P(None, None, None, ("space", "bead"))
    noise = P(None, None, None, None, ("space", "bead"))
    return jax.shard_map(
        on_device, mesh=mesh, in_specs=(wide, wide, wide, P(), P(), aux, noise),
        out_specs=(wide, wide, wide, aux), check_vma=False,
    )
```

```python
import math

import jax
import jax.numpy as jnp
import numpy as np
from jax import lax
from jax.experimental import pallas as pl
from jax.experimental.pallas import tpu as pltpu
from jax.sharding import PartitionSpec as P

BEADS, OWNERS, SPACES, CELL, AUX, STEPS = 32, 32, 4, 128, 4, 2
TIME_STEP, FREQ, LENGTH, STRENGTH = 0.5, 1.5, 2.0, 0.1
HALF = 0.5 * TIME_STEP
SCALE = math.sqrt(math.log2(math.e))
SHIFT = LENGTH * SCALE
F32, BF16 = jnp.float32, jnp.bfloat16
MESH = pl.DeviceIdType.MESH
HIGHEST = lax.Precision.HIGHEST
AHEAD = 1
CHUNKS = 1
PART = BEADS // CHUNKS
ORDER1, ORDER2 = (2, 1, 3, 0), (0, 1, 3, 2)


def constants():
    j = np.arange(BEADS, dtype=np.float64)
    phase = 2.0 * np.pi * j[:, None] * j[None, :] / BEADS
    k = j[None, :]
    basis = np.where(k < BEADS // 2, np.sqrt(2.0 / BEADS) * np.cos(phase), np.sqrt(2.0 / BEADS) * np.sin(phase))
    basis = np.where(k == 0, np.sqrt(1.0 / BEADS), basis)
    basis = np.where(k == BEADS // 2, np.sqrt(1.0 / BEADS) * np.cos(np.pi * j[:, None]), basis)
    freq = 2.0 * FREQ * np.sin(np.pi * j / BEADS)
    safe = np.where(j == 0, 1.0, freq)
    sinc = np.where(j == 0, TIME_STEP, np.sin(TIME_STEP * freq) / safe)
    out = np.zeros((5, BEADS, CELL), np.float32)
    out[0, :, :BEADS] = basis.T
    out[1, :, :BEADS] = basis
    out[2] = np.cos(TIME_STEP * freq)[:, None]
    out[3] = sinc[:, None]
    out[4] = (freq * np.sin(TIME_STEP * freq))[:, None]
    return out


def split3(x):
    a = x.astype(BF16).astype(F32)
    r = x - a
    b = r.astype(BF16).astype(F32)
    return a, b, r - b


NN = (((1,), (0,)), ((), ()))


def exponents(xs, yss):
    none = jnp.zeros((48, CELL), BF16)
    sides = []
    for x in xs:
        a, b, c = split3(x)
        sides.append(jnp.concatenate([a, a, b, b, a, c], axis=0).astype(BF16))
    right = jnp.concatenate(
        [jnp.concatenate([sides[0], none], axis=1), jnp.concatenate([none, sides[1]], axis=1)], axis=0
    )
    rows, left = [], []
    for k in range(len(yss[0])):
        parts = [split3(ys[k]) for ys in yss]
        rows.append(jnp.concatenate([v for a, b, c in parts for v in (a, b, a, b, c, a)], axis=0).T.astype(BF16))
        left += [jnp.concatenate([v for a, b, _ in parts for v in (a, b)], axis=0).astype(BF16)] * 2
    e = lax.dot_general(jnp.concatenate(rows, axis=0), right, NN, preferred_element_type=F32)
    return e, jnp.concatenate(left, axis=1)


def pulls(e, left):
    parts = []
    for k in range(e.shape[0] // CELL):
        w = jnp.exp2(e[k * CELL : (k + 1) * CELL])
        hi = w.astype(BF16)
        parts += [hi, (w - hi.astype(F32)).astype(BF16)]
    o = lax.dot_general(left, jnp.concatenate(parts, axis=0), NN, preferred_element_type=F32)
    own = [o[16 * k : 16 * k + 16, CELL * k : CELL * k + CELL] for k in range(2)]
    return [v[:8] + v[8:] for v in own]


def pipelined(cells, x_of, ys_of, done):
    cells, todo = list(cells), []
    pairs = [cells[i : i + 2] for i in range(0, len(cells), 2)]
    for i in range(len(pairs) + AHEAD):
        if i < len(pairs):
            todo.append(exponents([x_of(c) for c in pairs[i]], [ys_of(c) for c in pairs[i]]))
        if i >= AHEAD:
            for c, v in zip(pairs[i - AHEAD], pulls(*todo[i - AHEAD])):
                done(c, v)


def put_fixed(px, others):
    one, zero = jnp.ones((65, CELL), F32), jnp.zeros((65, CELL), F32)
    for ref, row in [(px, 4)] + [(r, 3) for r in others]:
        for r in (row, 5, 6, 7):
            ref[pl.ds(r, 65, stride=8), :] = one if r == row else zero


def put_points(ref, base, tiles, shift, center):
    n = tiles[0].shape[0]
    t = [tiles[0] + shift, tiles[1], tiles[2]] if shift else list(tiles)
    norm = -0.5 * (t[0] * t[0] + t[1] * t[1] + t[2] * t[2])
    for r, v in enumerate(t):
        ref[pl.ds(base + r, n, stride=8), :] = v
    ref[pl.ds(base + (3 if center else 4), n, stride=8), :] = norm


def at(c):
    return pl.ds(pl.multiple_of(c * 8, 8), 8)


def force_of(x, s):
    return (STRENGTH / SCALE) * (x * s[3:4] - s)


def own_cells(px, p0, fb):
    def done(c, v):
        fb[at(c), :] = v

    pipelined(range(64), lambda c: px[at(c), :], lambda c: [p0[at(c), :]], done)


def next_cells(cells, px, pm, pp, fb):
    def done(c, v):
        fb[at(c), :] = force_of(px[at(c), :], fb[at(c), :] + v)

    pipelined(cells, lambda c: px[at(c), :], lambda c: [pm[at(c), :], pp[at(c), :]], done)


def three_cells(cells, px, pm, p0, pp, fb):
    def done(c, v):
        fb[at(c), :] = force_of(px[at(c), :], v)

    pipelined(cells, lambda c: px[at(c), :], lambda c: [pm[at(c), :], p0[at(c), :], pp[at(c + 1), :]], done)


TILES = [(c, h) for c in range(3) for h in range(2)]


def mm(a, b):
    return jnp.dot(a, b, precision=HIGHEST, preferred_element_type=F32)


def exchange(me, send, recv, ssem, rsem, first, rows, order):
    plane, place = me // 8, lax.rem(me, 8)

    def copy(peer, slot):
        return pltpu.make_async_remote_copy(
            src_ref=send.at[pl.ds(pl.multiple_of(peer * 16 + first, 8), rows)],
            dst_ref=recv.at[pl.ds(pl.multiple_of(slot * 16 + first, 8), rows)],
            send_sem=ssem.at[peer],
            recv_sem=rsem.at[slot],
            device_id={"bead": peer},
            device_id_type=MESH,
        )

    def each(step, act):
        base = lax.rem(plane + step, 4) * 8

        def one(k, carry):
            act(base + lax.rem(place + k, 8))
            return carry

        lax.fori_loop(0 if step else 1, 8, one, 0)

    for step in order:
        each(step, lambda peer: copy(peer, me).start())
    own = pl.ds(pl.multiple_of(me * 16 + first, 8), 8 * (1 + rows // 8))
    recv[own, :] = send[own, :]

    def arrived(step):
        each(step, lambda peer: copy(peer, peer).wait_recv())

    def sent():
        for step in order:
            each(step, lambda peer: copy(peer, me).wait_send())

    return arrived, sent


def body(
    q_hbm, p_hbm, f_hbm, dr_hbm, mx_hbm, aux_hbm, noise_hbm, cst_hbm,
    q_out, p_out, f_out, aux_out,
    q, p, f, dr, mx, aux, noise, cst,
    send, recv, send2, recv2, edge, coef, u, u2, hs, hr,
    px, pm, p0, pp, fb,
    lsem, s1, r1, s2, r2, s3, r3, hssem, hrsem, essem, ersem,
):
    s, me = lax.axis_index("space"), lax.axis_index("bead")
    loads = [
        pltpu.make_async_copy(a, b, lsem.at[i])
        for i, (a, b) in enumerate(
            [(q_hbm, q), (p_hbm, p), (f_hbm, f), (dr_hbm, dr), (mx_hbm, mx), (aux_hbm, aux), (noise_hbm, noise), (cst_hbm, cst)]
        )
    ]
    for c in loads:
        c.start()
    barrier = pltpu.get_barrier_semaphore()
    up, down = lax.rem(s + 1, SPACES), lax.rem(s + SPACES - 1, SPACES)

    def greet(k, carry):
        pl.semaphore_signal(barrier, inc=1, device_id={"bead": lax.rem(me + k, OWNERS)}, device_id_type=MESH)
        return carry

    lax.fori_loop(1, OWNERS, greet, 0)

    first, last = me == 0, me == OWNERS - 1

    @pl.when(jnp.logical_or(first, last))
    def _():
        there, bead = jnp.where(first, down, up), OWNERS - 1 - me
        pl.semaphore_signal(barrier, inc=1, device_id={"space": there, "bead": bead}, device_id_type=MESH)

    for c in loads[:3]:
        c.wait()
    for h in range(2):
        for c in range(3):
            rows = pl.ds(h * 32, 32)
            send[pl.ds(h * 3 + c, 32, stride=16), :] = q[c, rows, :]
            send[pl.ds(6 + h * 3 + c, 32, stride=16), :] = p[c, rows, :] + HALF * f[c, rows, :]
    put_fixed(px, (pm, p0, pp))
    pl.semaphore_wait(barrier, OWNERS - 1 + jnp.where(jnp.logical_or(first, last), 1, 0))
    arrived, sent = exchange(me, send, recv, s1, r1, 0, 12, ORDER1)

    for c in loads[3:]:
        c.wait()
    for m, ref in enumerate((dr, mx)):
        for a in range(5):
            cols = ref[a].T
            for b in range(5):
                coef[m, a, b] = jnp.broadcast_to(cols[:, b : b + 1], (BEADS, CELL))
    for t, (c, h) in enumerate(TILES):
        lanes = pl.ds(t * CELL, CELL)
        state = [aux[pl.ds(c * 8 + h * 4 + a, 32, stride=24), :] for a in range(AUX)]
        kick = [[noise[st, b, c, :, pl.ds(h * CELL, CELL)] for b in range(5)] for st in range(STEPS)]
        for a in range(5):
            total = coef[1, a, 0] * kick[0][0]
            later = coef[1, a, 0] * kick[1][0]
            for b in range(1, 5):
                total = total + coef[1, a, b] * kick[0][b]
                later = later + coef[1, a, b] * kick[1][b]
            for b in range(AUX):
                total = total + coef[0, a, b + 1] * state[b]
            u[a, :, lanes] = total
            u2[a, :, lanes] = later

    for step in range(4):
        arrived(step)
    fwd, inv = cst[0][:, :BEADS], cst[1][:, :BEADS]
    wide = lambda v: jnp.concatenate([v] * 6, axis=1)
    cosine, sinc, wsin = wide(cst[2]), wide(cst[3]), wide(cst[4])
    drift0 = [wide(coef[0, a, 0]) for a in range(5)]

    def free(qm, pm_, kick):
        z = drift0[0] * pm_ + kick[0]
        rest = [drift0[a] * pm_ + kick[a] for a in range(1, 5)]
        return qm * cosine + sinc * z, z * cosine - wsin * qm, rest

    qm = mm(fwd, jnp.concatenate([recv[pl.ds(h * 3 + c, 32, stride=16), :] for c, h in TILES], axis=1))
    pmode = mm(fwd, jnp.concatenate([recv[pl.ds(6 + h * 3 + c, 32, stride=16), :] for c, h in TILES], axis=1))
    qm, pmode, state = free(qm, pmode, u)
    points = mm(inv, qm) * SCALE
    tile = lambda v, c, h: v[:, (2 * c + h) * CELL : (2 * c + h + 1) * CELL]
    for h in range(2):
        for c in range(3):
            hs[h, c] = tile(points, c, h)

    halo = []
    for k in range(CHUNKS):
        beads = pl.ds(k * PART, PART)
        for h in range(2):
            mine = s * 64 + h * 32 + me
            for side, step in ((0, 1), (1, 255)):
                there = lax.rem(mine + step, 256)
                slot = lax.rem(there // 32, 2)
                halo.append(
                    pltpu.make_async_remote_copy(
                        src_ref=hs.at[h, :, beads],
                        dst_ref=hr.at[side, slot, :, beads],
                        send_sem=hssem.at[k, side, h],
                        recv_sem=hrsem.at[k, side, slot],
                        device_id={"space": there // 64, "bead": lax.rem(there, 32)},
                        device_id_type=MESH,
                    )
                )
    for c in halo:
        c.start()
    for h in range(2):
        mine = [tile(points, c, h) for c in range(3)]
        put_points(px, h * 256, mine, 0.0, True)
        put_points(p0, h * 256, mine, 0.0, False)
    for a in range(5):
        total = u2[a]
        for b in range(AUX):
            total = total + wide(coef[0, a, b + 1]) * state[b]
        u2[a] = total
    own_cells(px, p0, fb)
    for k in range(CHUNKS):
        beads = pl.ds(k * PART, PART)
        for side, (ref, shift) in enumerate(((pm, -SHIFT), (pp, SHIFT))):
            for h in range(2):
                pltpu.make_async_remote_copy(
                    src_ref=hs.at[h, :, beads], dst_ref=hr.at[side, h, :, beads],
                    send_sem=hssem.at[k, side, h], recv_sem=hrsem.at[k, side, h],
                    device_id={"space": up}, device_id_type=MESH,
                ).wait_recv()
                put_points(ref, h * 256 + k * PART * 8, [hr[side, h, c, beads, :] for c in range(3)], shift, False)
        next_cells([h * 32 + k * PART + i for h in range(2) for i in range(PART)], px, pm, pp, fb)
    force = jnp.concatenate([fb[pl.ds(h * 256 + c, 32, stride=8), :] for c, h in TILES], axis=1)
    pmode = pmode + 2.0 * HALF * mm(fwd, force)
    qm, pmode, state = free(qm, pmode, u2)
    qb = mm(inv, qm)
    for c, h in TILES:
        send2[pl.ds(h * 3 + c, 32, stride=16), :] = tile(qb, c, h)
    arrived2, sent2 = exchange(me, send2, recv2, s2, r2, 0, 6, ORDER2)

    def edge_copy(side, bead):
        return pltpu.make_async_remote_copy(
            src_ref=send2.at[pl.ds(pl.multiple_of(bead * 16, 16), 6)],
            dst_ref=edge.at[pl.ds(side * 8, 6)],
            send_sem=essem.at[bead],
            recv_sem=ersem.at[side],
            device_id={"space": (up, down)[side], "bead": bead},
            device_id_type=MESH,
        )

    def edge_owners(act):
        for side, owner in ((0, last), (1, first)):

            @pl.when(owner)
            def _():
                def one(k, carry):
                    act(edge_copy(side, lax.rem(me + k, OWNERS)))
                    return carry

                lax.fori_loop(0, OWNERS, one, 0)

    edge_owners(lambda copy: copy.start())
    pb = mm(inv, pmode)
    for c, h in TILES:
        send2[pl.ds(8 + h * 3 + c, 32, stride=16), :] = tile(pb, c, h)
    arrived3, sent3 = exchange(me, send2, recv2, s3, r3, 8, 6, ORDER2)
    for c, h in TILES:
        for a in range(AUX):
            aux_out[pl.ds(c * 8 + h * 4 + a, 32, stride=24), :] = tile(state[a], c, h)
    for c in halo:
        c.wait_send()
    sent()
    plane = me // 8
    for step in range(4):
        arrived2(step)
    for h in range(2):
        tiles = [recv2[pl.ds(h * 3 + c, 32, stride=16), :] * SCALE for c in range(3)]
        put_points(px, h * 256, tiles, 0.0, True)
        put_points(p0, h * 256, tiles, 0.0, False)
        put_points(pm, h * 256 + 8, tiles, -SHIFT, False)
        put_points(pp, h * 256, tiles, SHIFT, False)
    three_cells(range(1, 63), px, pm, p0, pp, fb)
    for side in range(2):
        edge_copy(side, 0).wait_recv()
    put_points(pm, 0, [edge[3 + c : 4 + c, :] * SCALE for c in range(3)], -SHIFT, False)
    put_points(pp, 512, [edge[8 + c : 9 + c, :] * SCALE for c in range(3)], SHIFT, False)
    three_cells((0, 63), px, pm, p0, pp, fb)
    for step in range(4):
        arrived3(step)
    for h in range(2):
        rows = pl.ds(h * 32, 32)
        for c in range(3):
            force = fb[pl.ds(h * 256 + c, 32, stride=8), :]
            f_out[c, rows, :] = force
            q_out[c, rows, :] = recv2[pl.ds(h * 3 + c, 32, stride=16), :]
            p_out[c, rows, :] = recv2[pl.ds(8 + h * 3 + c, 32, stride=16), :] + HALF * force
    edge_owners(lambda copy: copy.wait_send())
    sent2()
    sent3()


def hand_over(*refs):
    copies = [pltpu.make_async_copy(refs[i], refs[4 + i], refs[8].at[i]) for i in range(4)]
    for c in copies:
        c.start()
    for c in copies:
        c.wait()


def on_device(positions, momenta, forces, gle_drift, gle_noise_mix, aux_momenta, noise):
    cells = lambda v: v.reshape(3, 64, CELL)
    modes_last = lambda v: jnp.transpose(v, (1, 2, 0))
    aux = jnp.transpose(aux_momenta.reshape(BEADS, AUX, 3, 2, CELL), (0, 2, 3, 1, 4)).reshape(768, CELL)
    kicks = jnp.transpose(noise, (0, 2, 3, 1, 4))
    big = jax.ShapeDtypeStruct((3, 64, CELL), F32)
    vm = lambda *shape: pltpu.VMEM(shape, F32)
    dma = lambda *shape: pltpu.SemaphoreType.DMA(shape)
    any_, vmem = pl.BlockSpec(memory_space=pl.ANY), pl.BlockSpec(memory_space=pltpu.VMEM)
    shapes = ((3, 64, CELL),) * 3 + ((768, CELL),)
    results = pl.pallas_call(
        body,
        out_shape=tuple(pltpu.VMEM(x, F32) for x in shapes),
        in_specs=[any_] * 8,
        out_specs=(vmem,) * 4,
        scratch_shapes=[
            vm(3, 64, CELL), vm(3, 64, CELL), vm(3, 64, CELL), vm(5, 5, BEADS), vm(5, 5, BEADS),
            vm(768, CELL), vm(2, 5, 3, BEADS, 256), vm(5, BEADS, CELL),
            vm(512, CELL), vm(512, CELL), vm(512, CELL), vm(512, CELL), vm(16, CELL),
            vm(2, 5, 5, BEADS, CELL), vm(5, BEADS, 768), vm(5, BEADS, 768),
            vm(2, 3, BEADS, CELL), vm(2, 2, 3, BEADS, CELL),
            *([vm(520, CELL)] * 5),
            dma(8), *([dma(OWNERS)] * 6), dma(CHUNKS, 2, 2), dma(CHUNKS, 2, 2), dma(OWNERS), dma(2),
        ],
        compiler_params=pltpu.CompilerParams(collective_id=0, has_side_effects=True),
    )(cells(positions), cells(momenta), cells(forces), modes_last(gle_drift), modes_last(gle_noise_mix), aux, kicks, jnp.asarray(constants()))
    q, p, f, a = pl.pallas_call(
        hand_over,
        out_shape=tuple(jax.ShapeDtypeStruct(x, F32) for x in shapes),
        in_specs=[any_] * 4,
        out_specs=(any_,) * 4,
        scratch_shapes=[dma(4)],
    )(*[pltpu.with_memory_space_constraint(x, pltpu.VMEM) for x in results])
    aux_new = jnp.transpose(a.reshape(BEADS, 3, 2, AUX, CELL), (0, 3, 1, 2, 4)).reshape(BEADS, AUX, 3, 256)
    back = lambda v: v.reshape(1, 3, 8192)
    return back(q), back(p), back(f), aux_new


def solution(mesh):
    wide = P("bead", None, "space")
    aux = P(None, None, None, ("space", "bead"))
    noise = P(None, None, None, None, ("space", "bead"))
    return jax.shard_map(
        on_device, mesh=mesh, in_specs=(wide, wide, wide, P(), P(), aux, noise),
        out_specs=(wide, wide, wide, aux), check_vma=False,
    )
```

```python
import math

import jax
import jax.numpy as jnp
import numpy as np
from jax import lax
from jax.experimental import pallas as pl
from jax.experimental.pallas import tpu as pltpu
from jax.sharding import PartitionSpec as P

BEADS, OWNERS, SPACES, CELL, AUX, STEPS = 32, 32, 4, 128, 4, 2
TIME_STEP, FREQ, LENGTH, STRENGTH = 0.5, 1.5, 2.0, 0.1
HALF = 0.5 * TIME_STEP
SCALE = math.sqrt(math.log2(math.e))
SHIFT = LENGTH * SCALE
F32, BF16 = jnp.float32, jnp.bfloat16
MESH = pl.DeviceIdType.MESH
HIGHEST = lax.Precision.HIGHEST
AHEAD = 1
CHUNKS = 1
PART = BEADS // CHUNKS
ORDER1, ORDER2 = (2, 1, 3, 0), (2, 1, 3, 0)


def constants():
    j = np.arange(BEADS, dtype=np.float64)
    phase = 2.0 * np.pi * j[:, None] * j[None, :] / BEADS
    k = j[None, :]
    basis = np.where(k < BEADS // 2, np.sqrt(2.0 / BEADS) * np.cos(phase), np.sqrt(2.0 / BEADS) * np.sin(phase))
    basis = np.where(k == 0, np.sqrt(1.0 / BEADS), basis)
    basis = np.where(k == BEADS // 2, np.sqrt(1.0 / BEADS) * np.cos(np.pi * j[:, None]), basis)
    freq = 2.0 * FREQ * np.sin(np.pi * j / BEADS)
    safe = np.where(j == 0, 1.0, freq)
    sinc = np.where(j == 0, TIME_STEP, np.sin(TIME_STEP * freq) / safe)
    out = np.zeros((5, BEADS, CELL), np.float32)
    out[0, :, :BEADS] = basis.T
    out[1, :, :BEADS] = basis
    out[2] = np.cos(TIME_STEP * freq)[:, None]
    out[3] = sinc[:, None]
    out[4] = (freq * np.sin(TIME_STEP * freq))[:, None]
    return out


def split3(x):
    a = x.astype(BF16).astype(F32)
    r = x - a
    b = r.astype(BF16).astype(F32)
    return a, b, r - b


NN = (((1,), (0,)), ((), ()))


def exponents(xs, yss):
    none = jnp.zeros((48, CELL), BF16)
    sides = []
    for x in xs:
        a, b, c = split3(x)
        sides.append(jnp.concatenate([a, a, b, b, a, c], axis=0).astype(BF16))
    right = jnp.concatenate(
        [jnp.concatenate([sides[0], none], axis=1), jnp.concatenate([none, sides[1]], axis=1)], axis=0
    )
    rows, left = [], []
    for k in range(len(yss[0])):
        parts = [split3(ys[k]) for ys in yss]
        rows.append(jnp.concatenate([v for a, b, c in parts for v in (a, b, a, b, c, a)], axis=0).T.astype(BF16))
        left += [jnp.concatenate([v for a, b, _ in parts for v in (a, b)], axis=0).astype(BF16)] * 2
    e = lax.dot_general(jnp.concatenate(rows, axis=0), right, NN, preferred_element_type=F32)
    return e, jnp.concatenate(left, axis=1)


def pulls(e, left):
    parts = []
    for k in range(e.shape[0] // CELL):
        w = jnp.exp2(e[k * CELL : (k + 1) * CELL])
        hi = w.astype(BF16)
        parts += [hi, (w - hi.astype(F32)).astype(BF16)]
    o = lax.dot_general(left, jnp.concatenate(parts, axis=0), NN, preferred_element_type=F32)
    own = [o[16 * k : 16 * k + 16, CELL * k : CELL * k + CELL] for k in range(2)]
    return [v[:8] + v[8:] for v in own]


def pipelined(cells, x_of, ys_of, done):
    cells, todo = list(cells), []
    pairs = [cells[i : i + 2] for i in range(0, len(cells), 2)]
    for i in range(len(pairs) + AHEAD):
        if i < len(pairs):
            todo.append(exponents([x_of(c) for c in pairs[i]], [ys_of(c) for c in pairs[i]]))
        if i >= AHEAD:
            for c, v in zip(pairs[i - AHEAD], pulls(*todo[i - AHEAD])):
                done(c, v)


def put_fixed(px, others):
    one, zero = jnp.ones((65, CELL), F32), jnp.zeros((65, CELL), F32)
    for ref, row in [(px, 4)] + [(r, 3) for r in others]:
        for r in (row, 5, 6, 7):
            ref[pl.ds(r, 65, stride=8), :] = one if r == row else zero


def put_points(ref, base, tiles, shift, center):
    n = tiles[0].shape[0]
    t = [tiles[0] + shift, tiles[1], tiles[2]] if shift else list(tiles)
    norm = -0.5 * (t[0] * t[0] + t[1] * t[1] + t[2] * t[2])
    for r, v in enumerate(t):
        ref[pl.ds(base + r, n, stride=8), :] = v
    ref[pl.ds(base + (3 if center else 4), n, stride=8), :] = norm


def at(c):
    return pl.ds(pl.multiple_of(c * 8, 8), 8)


def force_of(x, s):
    return (STRENGTH / SCALE) * (x * s[3:4] - s)


def own_cells(px, p0, fb):
    def done(c, v):
        fb[at(c), :] = v

    pipelined(range(64), lambda c: px[at(c), :], lambda c: [p0[at(c), :]], done)


def next_cells(cells, px, pm, pp, fb):
    def done(c, v):
        fb[at(c), :] = force_of(px[at(c), :], fb[at(c), :] + v)

    pipelined(cells, lambda c: px[at(c), :], lambda c: [pm[at(c), :], pp[at(c), :]], done)


def three_cells(cells, px, pm, p0, pp, fb):
    def done(c, v):
        fb[at(c), :] = force_of(px[at(c), :], v)

    pipelined(cells, lambda c: px[at(c), :], lambda c: [pm[at(c), :], p0[at(c), :], pp[at(c + 1), :]], done)


TILES = [(c, h) for c in range(3) for h in range(2)]


def mm(a, b):
    return jnp.dot(a, b, precision=HIGHEST, preferred_element_type=F32)


def take(sem, like, rows):
    part = like.at[pl.ds(0, rows)]
    pltpu.make_async_copy(part, part, sem).wait()


def exchange(me, send, recv, ssem, rsem, first, rows, order):
    plane, place = me // 8, lax.rem(me, 8)
    for step in order:
        base = lax.rem(plane + step, 4) * 8
        for k in range(0 if step else 1, 8):
            peer = base + lax.rem(place + k, 8)
            pltpu.make_async_remote_copy(
                src_ref=send.at[pl.ds(pl.multiple_of(peer * 16 + first, 8), rows)],
                dst_ref=recv.at[pl.ds(pl.multiple_of(me * 16 + first, 8), rows)],
                send_sem=ssem,
                recv_sem=rsem,
                device_id={"bead": peer},
                device_id_type=MESH,
            ).start()
    own = pl.ds(pl.multiple_of(me * 16 + first, 8), 8 * (1 + rows // 8))
    recv[own, :] = send[own, :]
    total = (OWNERS - 1) * rows
    return (lambda: take(rsem, recv, total)), (lambda: take(ssem, send, total))


def body(
    q_hbm, p_hbm, f_hbm, dr_hbm, mx_hbm, aux_hbm, noise_hbm, cst_hbm,
    q_out, p_out, f_out, aux_out,
    q, p, f, dr, mx, aux, noise, cst,
    send, recv, send2, recv2, edge, coef, u, u2, hs, hr,
    px, pm, p0, pp, fb,
    lsem, ssem, rsem, hssem, hrsem, essem, ersem,
):
    s, me = lax.axis_index("space"), lax.axis_index("bead")
    loads = [
        pltpu.make_async_copy(a, b, lsem.at[i])
        for i, (a, b) in enumerate(
            [(q_hbm, q), (p_hbm, p), (f_hbm, f), (dr_hbm, dr), (mx_hbm, mx), (aux_hbm, aux), (noise_hbm, noise), (cst_hbm, cst)]
        )
    ]
    for c in loads:
        c.start()
    barrier = pltpu.get_barrier_semaphore()
    up, down = lax.rem(s + 1, SPACES), lax.rem(s + SPACES - 1, SPACES)

    for k in range(1, OWNERS):
        pl.semaphore_signal(barrier, inc=1, device_id={"bead": lax.rem(me + k, OWNERS)}, device_id_type=MESH)

    first, last = me == 0, me == OWNERS - 1

    @pl.when(jnp.logical_or(first, last))
    def _():
        there, bead = jnp.where(first, down, up), OWNERS - 1 - me
        pl.semaphore_signal(barrier, inc=1, device_id={"space": there, "bead": bead}, device_id_type=MESH)

    for c in loads[:3]:
        c.wait()
    for h in range(2):
        for c in range(3):
            rows = pl.ds(h * 32, 32)
            send[pl.ds(h * 3 + c, 32, stride=16), :] = q[c, rows, :]
            send[pl.ds(6 + h * 3 + c, 32, stride=16), :] = p[c, rows, :] + HALF * f[c, rows, :]
    put_fixed(px, (pm, p0, pp))
    pl.semaphore_wait(barrier, OWNERS - 1 + jnp.where(jnp.logical_or(first, last), 1, 0))
    arrived, sent = exchange(me, send, recv, ssem.at[0], rsem.at[0], 0, 12, ORDER1)

    for c in loads[3:]:
        c.wait()
    for m, ref in enumerate((dr, mx)):
        for a in range(5):
            cols = ref[a].T
            for b in range(5):
                coef[m, a, b] = jnp.broadcast_to(cols[:, b : b + 1], (BEADS, CELL))
    for t, (c, h) in enumerate(TILES):
        lanes = pl.ds(t * CELL, CELL)
        state = [aux[pl.ds(c * 8 + h * 4 + a, 32, stride=24), :] for a in range(AUX)]
        kick = [[noise[st, b, c, :, pl.ds(h * CELL, CELL)] for b in range(5)] for st in range(STEPS)]
        for a in range(5):
            total = coef[1, a, 0] * kick[0][0]
            later = coef[1, a, 0] * kick[1][0]
            for b in range(1, 5):
                total = total + coef[1, a, b] * kick[0][b]
                later = later + coef[1, a, b] * kick[1][b]
            for b in range(AUX):
                total = total + coef[0, a, b + 1] * state[b]
            u[a, :, lanes] = total
            u2[a, :, lanes] = later

    arrived()
    fwd, inv = cst[0][:, :BEADS], cst[1][:, :BEADS]
    wide = lambda v: jnp.concatenate([v] * 6, axis=1)
    cosine, sinc, wsin = wide(cst[2]), wide(cst[3]), wide(cst[4])
    drift0 = [wide(coef[0, a, 0]) for a in range(5)]

    def free(qm, pm_, kick):
        z = drift0[0] * pm_ + kick[0]
        rest = [drift0[a] * pm_ + kick[a] for a in range(1, 5)]
        return qm * cosine + sinc * z, z * cosine - wsin * qm, rest

    qm = mm(fwd, jnp.concatenate([recv[pl.ds(h * 3 + c, 32, stride=16), :] for c, h in TILES], axis=1))
    pmode = mm(fwd, jnp.concatenate([recv[pl.ds(6 + h * 3 + c, 32, stride=16), :] for c, h in TILES], axis=1))
    qm, pmode, state = free(qm, pmode, u)
    points = mm(inv, qm) * SCALE
    tile = lambda v, c, h: v[:, (2 * c + h) * CELL : (2 * c + h + 1) * CELL]
    for h in range(2):
        for c in range(3):
            hs[h, c] = tile(points, c, h)

    halo = []
    for k in range(CHUNKS):
        beads = pl.ds(k * PART, PART)
        for h in range(2):
            mine = s * 64 + h * 32 + me
            for side, step in ((0, 1), (1, 255)):
                there = lax.rem(mine + step, 256)
                slot = lax.rem(there // 32, 2)
                halo.append(
                    pltpu.make_async_remote_copy(
                        src_ref=hs.at[h, :, beads],
                        dst_ref=hr.at[side, slot, :, beads],
                        send_sem=hssem.at[k, side, h],
                        recv_sem=hrsem.at[k, side, slot],
                        device_id={"space": there // 64, "bead": lax.rem(there, 32)},
                        device_id_type=MESH,
                    )
                )
    for c in halo:
        c.start()
    for h in range(2):
        mine = [tile(points, c, h) for c in range(3)]
        put_points(px, h * 256, mine, 0.0, True)
        put_points(p0, h * 256, mine, 0.0, False)
    for a in range(5):
        total = u2[a]
        for b in range(AUX):
            total = total + wide(coef[0, a, b + 1]) * state[b]
        u2[a] = total
    own_cells(px, p0, fb)
    for k in range(CHUNKS):
        beads = pl.ds(k * PART, PART)
        for side, (ref, shift) in enumerate(((pm, -SHIFT), (pp, SHIFT))):
            for h in range(2):
                pltpu.make_async_remote_copy(
                    src_ref=hs.at[h, :, beads], dst_ref=hr.at[side, h, :, beads],
                    send_sem=hssem.at[k, side, h], recv_sem=hrsem.at[k, side, h],
                    device_id={"space": up}, device_id_type=MESH,
                ).wait_recv()
                put_points(ref, h * 256 + k * PART * 8, [hr[side, h, c, beads, :] for c in range(3)], shift, False)
        next_cells([h * 32 + k * PART + i for h in range(2) for i in range(PART)], px, pm, pp, fb)
    force = jnp.concatenate([fb[pl.ds(h * 256 + c, 32, stride=8), :] for c, h in TILES], axis=1)
    pmode = pmode + 2.0 * HALF * mm(fwd, force)
    qm, pmode, state = free(qm, pmode, u2)
    qb = mm(inv, qm)
    for c, h in TILES:
        send2[pl.ds(h * 3 + c, 32, stride=16), :] = tile(qb, c, h)
    arrived2, sent2 = exchange(me, send2, recv2, ssem.at[1], rsem.at[1], 0, 6, ORDER2)

    def edge_copy(side, bead):
        return pltpu.make_async_remote_copy(
            src_ref=send2.at[pl.ds(pl.multiple_of(bead * 16, 16), 6)],
            dst_ref=edge.at[pl.ds(side * 8, 6)],
            send_sem=essem.at[0],
            recv_sem=ersem.at[side],
            device_id={"space": (up, down)[side], "bead": bead},
            device_id_type=MESH,
        )

    def edge_owners(act):
        for side, owner in ((0, last), (1, first)):

            @pl.when(owner)
            def _():
                def one(k, carry):
                    act(edge_copy(side, lax.rem(me + k, OWNERS)))
                    return carry

                lax.fori_loop(0, OWNERS, one, 0)

    edge_owners(lambda copy: copy.start())
    pb = mm(inv, pmode)
    for c, h in TILES:
        send2[pl.ds(8 + h * 3 + c, 32, stride=16), :] = tile(pb, c, h)
    arrived3, sent3 = exchange(me, send2, recv2, ssem.at[2], rsem.at[2], 8, 6, ORDER2)
    for c, h in TILES:
        for a in range(AUX):
            aux_out[pl.ds(c * 8 + h * 4 + a, 32, stride=24), :] = tile(state[a], c, h)
    for c in halo:
        c.wait_send()
    sent()
    arrived2()
    for h in range(2):
        tiles = [recv2[pl.ds(h * 3 + c, 32, stride=16), :] * SCALE for c in range(3)]
        put_points(px, h * 256, tiles, 0.0, True)
        put_points(p0, h * 256, tiles, 0.0, False)
        put_points(pm, h * 256 + 8, tiles, -SHIFT, False)
        put_points(pp, h * 256, tiles, SHIFT, False)
    three_cells(range(1, 63), px, pm, p0, pp, fb)
    for side in range(2):
        edge_copy(side, 0).wait_recv()
    put_points(pm, 0, [edge[3 + c : 4 + c, :] * SCALE for c in range(3)], -SHIFT, False)
    put_points(pp, 512, [edge[8 + c : 9 + c, :] * SCALE for c in range(3)], SHIFT, False)
    three_cells((0, 63), px, pm, p0, pp, fb)
    arrived3()
    for h in range(2):
        rows = pl.ds(h * 32, 32)
        for c in range(3):
            force = fb[pl.ds(h * 256 + c, 32, stride=8), :]
            f_out[c, rows, :] = force
            q_out[c, rows, :] = recv2[pl.ds(h * 3 + c, 32, stride=16), :]
            p_out[c, rows, :] = recv2[pl.ds(8 + h * 3 + c, 32, stride=16), :] + HALF * force
    for owner in (last, first):

        @pl.when(owner)
        def _():
            take(essem.at[0], send2, OWNERS * 6)

    sent2()
    sent3()


def hand_over(*refs):
    copies = [pltpu.make_async_copy(refs[i], refs[4 + i], refs[8].at[i]) for i in range(4)]
    for c in copies:
        c.start()
    for c in copies:
        c.wait()


def on_device(positions, momenta, forces, gle_drift, gle_noise_mix, aux_momenta, noise):
    cells = lambda v: v.reshape(3, 64, CELL)
    modes_last = lambda v: jnp.transpose(v, (1, 2, 0))
    aux = jnp.transpose(aux_momenta.reshape(BEADS, AUX, 3, 2, CELL), (0, 2, 3, 1, 4)).reshape(768, CELL)
    kicks = jnp.transpose(noise, (0, 2, 3, 1, 4))
    big = jax.ShapeDtypeStruct((3, 64, CELL), F32)
    vm = lambda *shape: pltpu.VMEM(shape, F32)
    dma = lambda *shape: pltpu.SemaphoreType.DMA(shape)
    any_, vmem = pl.BlockSpec(memory_space=pl.ANY), pl.BlockSpec(memory_space=pltpu.VMEM)
    shapes = ((3, 64, CELL),) * 3 + ((768, CELL),)
    results = pl.pallas_call(
        body,
        out_shape=tuple(pltpu.VMEM(x, F32) for x in shapes),
        in_specs=[any_] * 8,
        out_specs=(vmem,) * 4,
        scratch_shapes=[
            vm(3, 64, CELL), vm(3, 64, CELL), vm(3, 64, CELL), vm(5, 5, BEADS), vm(5, 5, BEADS),
            vm(768, CELL), vm(2, 5, 3, BEADS, 256), vm(5, BEADS, CELL),
            vm(512, CELL), vm(512, CELL), vm(512, CELL), vm(512, CELL), vm(16, CELL),
            vm(2, 5, 5, BEADS, CELL), vm(5, BEADS, 768), vm(5, BEADS, 768),
            vm(2, 3, BEADS, CELL), vm(2, 2, 3, BEADS, CELL),
            *([vm(520, CELL)] * 5),
            dma(8), dma(3), dma(3), dma(CHUNKS, 2, 2), dma(CHUNKS, 2, 2), dma(1), dma(2),
        ],
        compiler_params=pltpu.CompilerParams(collective_id=0, has_side_effects=True),
    )(cells(positions), cells(momenta), cells(forces), modes_last(gle_drift), modes_last(gle_noise_mix), aux, kicks, jnp.asarray(constants()))
    q, p, f, a = pl.pallas_call(
        hand_over,
        out_shape=tuple(jax.ShapeDtypeStruct(x, F32) for x in shapes),
        in_specs=[any_] * 4,
        out_specs=(any_,) * 4,
        scratch_shapes=[dma(4)],
    )(*[pltpu.with_memory_space_constraint(x, pltpu.VMEM) for x in results])
    aux_new = jnp.transpose(a.reshape(BEADS, 3, 2, AUX, CELL), (0, 3, 1, 2, 4)).reshape(BEADS, AUX, 3, 256)
    back = lambda v: v.reshape(1, 3, 8192)
    return back(q), back(p), back(f), aux_new


def solution(mesh):
    wide = P("bead", None, "space")
    aux = P(None, None, None, ("space", "bead"))
    noise = P(None, None, None, None, ("space", "bead"))
    return jax.shard_map(
        on_device, mesh=mesh, in_specs=(wide, wide, wide, P(), P(), aux, noise),
        out_specs=(wide, wide, wide, aux), check_vma=False,
    )
```

```python
import math

import jax
import jax.numpy as jnp
import numpy as np
from jax import lax
from jax.experimental import pallas as pl
from jax.experimental.pallas import tpu as pltpu
from jax.sharding import PartitionSpec as P

BEADS, OWNERS, SPACES, CELL, AUX, STEPS = 32, 32, 4, 128, 4, 2
TIME_STEP, FREQ, LENGTH, STRENGTH = 0.5, 1.5, 2.0, 0.1
HALF = 0.5 * TIME_STEP
SCALE = math.sqrt(math.log2(math.e))
SHIFT = LENGTH * SCALE
F32, BF16 = jnp.float32, jnp.bfloat16
MESH = pl.DeviceIdType.MESH
HIGHEST = lax.Precision.HIGHEST
AHEAD = 1
STAGES = ((0,), (1, 3, 2))
CHUNKS = 1
PART = BEADS // CHUNKS
ORDER1, ORDER2 = (2, 1, 3, 0), (2, 1, 3, 0)


def constants():
    j = np.arange(BEADS, dtype=np.float64)
    phase = 2.0 * np.pi * j[:, None] * j[None, :] / BEADS
    k = j[None, :]
    basis = np.where(k < BEADS // 2, np.sqrt(2.0 / BEADS) * np.cos(phase), np.sqrt(2.0 / BEADS) * np.sin(phase))
    basis = np.where(k == 0, np.sqrt(1.0 / BEADS), basis)
    basis = np.where(k == BEADS // 2, np.sqrt(1.0 / BEADS) * np.cos(np.pi * j[:, None]), basis)
    freq = 2.0 * FREQ * np.sin(np.pi * j / BEADS)
    safe = np.where(j == 0, 1.0, freq)
    sinc = np.where(j == 0, TIME_STEP, np.sin(TIME_STEP * freq) / safe)
    out = np.zeros((5, BEADS, CELL), np.float32)
    out[0, :, :BEADS] = basis.T
    out[1, :, :BEADS] = basis
    out[2] = np.cos(TIME_STEP * freq)[:, None]
    out[3] = sinc[:, None]
    out[4] = (freq * np.sin(TIME_STEP * freq))[:, None]
    return out


def split3(x):
    a = x.astype(BF16).astype(F32)
    r = x - a
    b = r.astype(BF16).astype(F32)
    return a, b, r - b


NN = (((1,), (0,)), ((), ()))


def exponents(xs, yss):
    none = jnp.zeros((48, CELL), BF16)
    sides = []
    for x in xs:
        a, b, c = split3(x)
        sides.append(jnp.concatenate([a, a, b, b, a, c], axis=0).astype(BF16))
    right = jnp.concatenate(
        [jnp.concatenate([sides[0], none], axis=1), jnp.concatenate([none, sides[1]], axis=1)], axis=0
    )
    rows, left = [], []
    for k in range(len(yss[0])):
        parts = [split3(ys[k]) for ys in yss]
        rows.append(jnp.concatenate([v for a, b, c in parts for v in (a, b, a, b, c, a)], axis=0).T.astype(BF16))
        left += [jnp.concatenate([v for a, b, _ in parts for v in (a, b)], axis=0).astype(BF16)] * 2
    e = lax.dot_general(jnp.concatenate(rows, axis=0), right, NN, preferred_element_type=F32)
    return e, jnp.concatenate(left, axis=1)


def pulls(e, left):
    parts = []
    for k in range(e.shape[0] // CELL):
        w = jnp.exp2(e[k * CELL : (k + 1) * CELL])
        hi = w.astype(BF16)
        parts += [hi, (w - hi.astype(F32)).astype(BF16)]
    o = lax.dot_general(left, jnp.concatenate(parts, axis=0), NN, preferred_element_type=F32)
    own = [o[16 * k : 16 * k + 16, CELL * k : CELL * k + CELL] for k in range(2)]
    return [v[:8] + v[8:] for v in own]


def pipelined(cells, x_of, ys_of, done):
    cells, todo = list(cells), []
    pairs = [cells[i : i + 2] for i in range(0, len(cells), 2)]
    for i in range(len(pairs) + AHEAD):
        if i < len(pairs):
            todo.append(exponents([x_of(c) for c in pairs[i]], [ys_of(c) for c in pairs[i]]))
        if i >= AHEAD:
            for c, v in zip(pairs[i - AHEAD], pulls(*todo[i - AHEAD])):
                done(c, v)


def put_fixed(px, others):
    one, zero = jnp.ones((65, CELL), F32), jnp.zeros((65, CELL), F32)
    for ref, row in [(px, 4)] + [(r, 3) for r in others]:
        for r in (row, 5, 6, 7):
            ref[pl.ds(r, 65, stride=8), :] = one if r == row else zero


def put_points(ref, base, tiles, shift, center):
    n = tiles[0].shape[0]
    t = [tiles[0] + shift, tiles[1], tiles[2]] if shift else list(tiles)
    norm = -0.5 * (t[0] * t[0] + t[1] * t[1] + t[2] * t[2])
    for r, v in enumerate(t):
        ref[pl.ds(base + r, n, stride=8), :] = v
    ref[pl.ds(base + (3 if center else 4), n, stride=8), :] = norm


def at(c):
    return pl.ds(pl.multiple_of(c * 8, 8), 8)


def force_of(x, s):
    return (STRENGTH / SCALE) * (x * s[3:4] - s)


def own_cells(px, p0, fb):
    def done(c, v):
        fb[at(c), :] = v

    pipelined(range(64), lambda c: px[at(c), :], lambda c: [p0[at(c), :]], done)


def next_cells(cells, px, pm, pp, fb):
    def done(c, v):
        fb[at(c), :] = force_of(px[at(c), :], fb[at(c), :] + v)

    pipelined(cells, lambda c: px[at(c), :], lambda c: [pm[at(c), :], pp[at(c), :]], done)


def three_cells(cells, px, pm, p0, pp, fb):
    def done(c, v):
        fb[at(c), :] = force_of(px[at(c), :], v)

    pipelined(cells, lambda c: px[at(c), :], lambda c: [pm[at(c), :], p0[at(c), :], pp[at(c + 1), :]], done)


TILES = [(c, h) for c in range(3) for h in range(2)]


def mm(a, b):
    return jnp.dot(a, b, precision=HIGHEST, preferred_element_type=F32)


def take(sem, like, rows):
    part = like.at[pl.ds(0, rows)]
    pltpu.make_async_copy(part, part, sem).wait()


def exchange(me, send, recv, ssem, rsem, first, rows, order, planes=None):
    plane, place = me // 8, lax.rem(me, 8)
    for step in order:
        base = lax.rem(plane + step, 4) * 8
        for k in range(0 if step else 1, 8):
            peer = base + lax.rem(place + k, 8)
            pltpu.make_async_remote_copy(
                src_ref=send.at[pl.ds(pl.multiple_of(peer * 16 + first, 8), rows)],
                dst_ref=recv.at[pl.ds(pl.multiple_of(me * 16 + first, 8), rows)],
                send_sem=ssem,
                recv_sem=rsem if planes is None else planes.at[plane],
                device_id={"bead": peer},
                device_id_type=MESH,
            ).start()
    own = pl.ds(pl.multiple_of(me * 16 + first, 8), 8 * (1 + rows // 8))
    recv[own, :] = send[own, :]
    total = (OWNERS - 1) * rows
    return (lambda: take(rsem, recv, total)), (lambda: take(ssem, send, total))


def body(
    q_hbm, p_hbm, f_hbm, dr_hbm, mx_hbm, aux_hbm, noise_hbm, cst_hbm,
    q_out, p_out, f_out, aux_out,
    q, p, f, dr, mx, aux, noise, cst,
    send, recv, send2, recv2, edge, coef, u, u2, hs, hr,
    px, pm, p0, pp, fb,
    lsem, ssem, rsem, psem, hssem, hrsem, essem, ersem,
):
    s, me = lax.axis_index("space"), lax.axis_index("bead")
    loads = [
        pltpu.make_async_copy(a, b, lsem.at[i])
        for i, (a, b) in enumerate(
            [(q_hbm, q), (p_hbm, p), (f_hbm, f), (dr_hbm, dr), (mx_hbm, mx), (aux_hbm, aux), (noise_hbm, noise), (cst_hbm, cst)]
        )
    ]
    for c in loads:
        c.start()
    barrier = pltpu.get_barrier_semaphore()
    up, down = lax.rem(s + 1, SPACES), lax.rem(s + SPACES - 1, SPACES)

    for k in range(1, OWNERS):
        pl.semaphore_signal(barrier, inc=1, device_id={"bead": lax.rem(me + k, OWNERS)}, device_id_type=MESH)

    first, last = me == 0, me == OWNERS - 1

    @pl.when(jnp.logical_or(first, last))
    def _():
        there, bead = jnp.where(first, down, up), OWNERS - 1 - me
        pl.semaphore_signal(barrier, inc=1, device_id={"space": there, "bead": bead}, device_id_type=MESH)

    for c in loads[:3]:
        c.wait()
    for h in range(2):
        for c in range(3):
            rows = pl.ds(h * 32, 32)
            send[pl.ds(h * 3 + c, 32, stride=16), :] = q[c, rows, :]
            send[pl.ds(6 + h * 3 + c, 32, stride=16), :] = p[c, rows, :] + HALF * f[c, rows, :]
    put_fixed(px, (pm, p0, pp))
    pl.semaphore_wait(barrier, OWNERS - 1 + jnp.where(jnp.logical_or(first, last), 1, 0))
    arrived, sent = exchange(me, send, recv, ssem.at[0], rsem.at[0], 0, 12, ORDER1)

    for c in loads[3:]:
        c.wait()
    for m, ref in enumerate((dr, mx)):
        for a in range(5):
            cols = ref[a].T
            for b in range(5):
                coef[m, a, b] = jnp.broadcast_to(cols[:, b : b + 1], (BEADS, CELL))
    for t, (c, h) in enumerate(TILES):
        lanes = pl.ds(t * CELL, CELL)
        state = [aux[pl.ds(c * 8 + h * 4 + a, 32, stride=24), :] for a in range(AUX)]
        kick = [[noise[st, b, c, :, pl.ds(h * CELL, CELL)] for b in range(5)] for st in range(STEPS)]
        for a in range(5):
            total = coef[1, a, 0] * kick[0][0]
            later = coef[1, a, 0] * kick[1][0]
            for b in range(1, 5):
                total = total + coef[1, a, b] * kick[0][b]
                later = later + coef[1, a, b] * kick[1][b]
            for b in range(AUX):
                total = total + coef[0, a, b + 1] * state[b]
            u[a, :, lanes] = total
            u2[a, :, lanes] = later

    arrived()
    fwd, inv = cst[0][:, :BEADS], cst[1][:, :BEADS]
    wide = lambda v: jnp.concatenate([v] * 6, axis=1)
    cosine, sinc, wsin = wide(cst[2]), wide(cst[3]), wide(cst[4])
    drift0 = [wide(coef[0, a, 0]) for a in range(5)]

    def free(qm, pm_, kick):
        z = drift0[0] * pm_ + kick[0]
        rest = [drift0[a] * pm_ + kick[a] for a in range(1, 5)]
        return qm * cosine + sinc * z, z * cosine - wsin * qm, rest

    qm = mm(fwd, jnp.concatenate([recv[pl.ds(h * 3 + c, 32, stride=16), :] for c, h in TILES], axis=1))
    pmode = mm(fwd, jnp.concatenate([recv[pl.ds(6 + h * 3 + c, 32, stride=16), :] for c, h in TILES], axis=1))
    qm, pmode, state = free(qm, pmode, u)
    points = mm(inv, qm) * SCALE
    tile = lambda v, c, h: v[:, (2 * c + h) * CELL : (2 * c + h + 1) * CELL]
    for h in range(2):
        for c in range(3):
            hs[h, c] = tile(points, c, h)

    halo = []
    for k in range(CHUNKS):
        beads = pl.ds(k * PART, PART)
        for h in range(2):
            mine = s * 64 + h * 32 + me
            for side, step in ((0, 1), (1, 255)):
                there = lax.rem(mine + step, 256)
                slot = lax.rem(there // 32, 2)
                halo.append(
                    pltpu.make_async_remote_copy(
                        src_ref=hs.at[h, :, beads],
                        dst_ref=hr.at[side, slot, :, beads],
                        send_sem=hssem.at[k, side, h],
                        recv_sem=hrsem.at[k, side, slot],
                        device_id={"space": there // 64, "bead": lax.rem(there, 32)},
                        device_id_type=MESH,
                    )
                )
    for c in halo:
        c.start()
    for h in range(2):
        mine = [tile(points, c, h) for c in range(3)]
        put_points(px, h * 256, mine, 0.0, True)
        put_points(p0, h * 256, mine, 0.0, False)
    for a in range(5):
        total = u2[a]
        for b in range(AUX):
            total = total + wide(coef[0, a, b + 1]) * state[b]
        u2[a] = total
    own_cells(px, p0, fb)
    for k in range(CHUNKS):
        beads = pl.ds(k * PART, PART)
        for side, (ref, shift) in enumerate(((pm, -SHIFT), (pp, SHIFT))):
            for h in range(2):
                pltpu.make_async_remote_copy(
                    src_ref=hs.at[h, :, beads], dst_ref=hr.at[side, h, :, beads],
                    send_sem=hssem.at[k, side, h], recv_sem=hrsem.at[k, side, h],
                    device_id={"space": up}, device_id_type=MESH,
                ).wait_recv()
                put_points(ref, h * 256 + k * PART * 8, [hr[side, h, c, beads, :] for c in range(3)], shift, False)
        next_cells([h * 32 + k * PART + i for h in range(2) for i in range(PART)], px, pm, pp, fb)
    force = jnp.concatenate([fb[pl.ds(h * 256 + c, 32, stride=8), :] for c, h in TILES], axis=1)
    pmode = pmode + 2.0 * HALF * mm(fwd, force)
    qm, pmode, state = free(qm, pmode, u2)
    qb = mm(inv, qm)
    for c, h in TILES:
        send2[pl.ds(h * 3 + c, 32, stride=16), :] = tile(qb, c, h)
    _, sent2 = exchange(me, send2, recv2, ssem.at[1], rsem.at[1], 0, 6, ORDER2, psem)

    def edge_copy(side, bead):
        return pltpu.make_async_remote_copy(
            src_ref=send2.at[pl.ds(pl.multiple_of(bead * 16, 16), 6)],
            dst_ref=edge.at[pl.ds(side * 8, 6)],
            send_sem=essem.at[0],
            recv_sem=ersem.at[side],
            device_id={"space": (up, down)[side], "bead": bead},
            device_id_type=MESH,
        )

    def edge_owners(act):
        for side, owner in ((0, last), (1, first)):

            @pl.when(owner)
            def _():
                def one(k, carry):
                    act(edge_copy(side, lax.rem(me + k, OWNERS)))
                    return carry

                lax.fori_loop(0, OWNERS, one, 0)

    edge_owners(lambda copy: copy.start())
    pb = mm(inv, pmode)
    for c, h in TILES:
        send2[pl.ds(8 + h * 3 + c, 32, stride=16), :] = tile(pb, c, h)
    arrived3, sent3 = exchange(me, send2, recv2, ssem.at[2], rsem.at[2], 8, 6, ORDER2)
    for c, h in TILES:
        for a in range(AUX):
            aux_out[pl.ds(c * 8 + h * 4 + a, 32, stride=24), :] = tile(state[a], c, h)
    for c in halo:
        c.wait_send()
    sent()
    plane = me // 8
    for steps in STAGES:
        inner = []
        for step in steps:
            here = lax.rem(plane + step, 4)
            take(psem.at[here], recv2, (8 if step else 7) * 6)
            for h in range(2):
                tiles = [recv2[pl.ds(here * 128 + h * 3 + c, 8, stride=16), :] * SCALE for c in range(3)]
                base = h * 256 + here * 64
                put_points(px, base, tiles, 0.0, True)
                put_points(p0, base, tiles, 0.0, False)
                put_points(pm, base + 8, tiles, -SHIFT, False)
                put_points(pp, base, tiles, SHIFT, False)
            inner += [h * 32 + here * 8 + i for h in range(2) for i in range(1, 7)]
        if steps is STAGES[-1]:
            inner += [8 * i + j for i in range(8) for j in (0, 7)][1:-1]
        three_cells(inner, px, pm, p0, pp, fb)
    for side in range(2):
        edge_copy(side, 0).wait_recv()
    put_points(pm, 0, [edge[3 + c : 4 + c, :] * SCALE for c in range(3)], -SHIFT, False)
    put_points(pp, 512, [edge[8 + c : 9 + c, :] * SCALE for c in range(3)], SHIFT, False)
    three_cells((0, 63), px, pm, p0, pp, fb)
    arrived3()
    for h in range(2):
        rows = pl.ds(h * 32, 32)
        for c in range(3):
            force = fb[pl.ds(h * 256 + c, 32, stride=8), :]
            f_out[c, rows, :] = force
            q_out[c, rows, :] = recv2[pl.ds(h * 3 + c, 32, stride=16), :]
            p_out[c, rows, :] = recv2[pl.ds(8 + h * 3 + c, 32, stride=16), :] + HALF * force
    for owner in (last, first):

        @pl.when(owner)
        def _():
            take(essem.at[0], send2, OWNERS * 6)

    sent2()
    sent3()


def hand_over(*refs):
    copies = [pltpu.make_async_copy(refs[i], refs[4 + i], refs[8].at[i]) for i in range(4)]
    for c in copies:
        c.start()
    for c in copies:
        c.wait()


def on_device(positions, momenta, forces, gle_drift, gle_noise_mix, aux_momenta, noise):
    cells = lambda v: v.reshape(3, 64, CELL)
    modes_last = lambda v: jnp.transpose(v, (1, 2, 0))
    aux = jnp.transpose(aux_momenta.reshape(BEADS, AUX, 3, 2, CELL), (0, 2, 3, 1, 4)).reshape(768, CELL)
    kicks = jnp.transpose(noise, (0, 2, 3, 1, 4))
    big = jax.ShapeDtypeStruct((3, 64, CELL), F32)
    vm = lambda *shape: pltpu.VMEM(shape, F32)
    dma = lambda *shape: pltpu.SemaphoreType.DMA(shape)
    any_, vmem = pl.BlockSpec(memory_space=pl.ANY), pl.BlockSpec(memory_space=pltpu.VMEM)
    shapes = ((3, 64, CELL),) * 3 + ((768, CELL),)
    results = pl.pallas_call(
        body,
        out_shape=tuple(pltpu.VMEM(x, F32) for x in shapes),
        in_specs=[any_] * 8,
        out_specs=(vmem,) * 4,
        scratch_shapes=[
            vm(3, 64, CELL), vm(3, 64, CELL), vm(3, 64, CELL), vm(5, 5, BEADS), vm(5, 5, BEADS),
            vm(768, CELL), vm(2, 5, 3, BEADS, 256), vm(5, BEADS, CELL),
            vm(512, CELL), vm(512, CELL), vm(512, CELL), vm(512, CELL), vm(16, CELL),
            vm(2, 5, 5, BEADS, CELL), vm(5, BEADS, 768), vm(5, BEADS, 768),
            vm(2, 3, BEADS, CELL), vm(2, 2, 3, BEADS, CELL),
            *([vm(520, CELL)] * 5),
            dma(8), dma(3), dma(3), dma(4), dma(CHUNKS, 2, 2), dma(CHUNKS, 2, 2), dma(1), dma(2),
        ],
        compiler_params=pltpu.CompilerParams(collective_id=0, has_side_effects=True),
    )(cells(positions), cells(momenta), cells(forces), modes_last(gle_drift), modes_last(gle_noise_mix), aux, kicks, jnp.asarray(constants()))
    q, p, f, a = pl.pallas_call(
        hand_over,
        out_shape=tuple(jax.ShapeDtypeStruct(x, F32) for x in shapes),
        in_specs=[any_] * 4,
        out_specs=(any_,) * 4,
        scratch_shapes=[dma(4)],
    )(*[pltpu.with_memory_space_constraint(x, pltpu.VMEM) for x in results])
    aux_new = jnp.transpose(a.reshape(BEADS, 3, 2, AUX, CELL), (0, 3, 1, 2, 4)).reshape(BEADS, AUX, 3, 256)
    back = lambda v: v.reshape(1, 3, 8192)
    return back(q), back(p), back(f), aux_new


def solution(mesh):
    wide = P("bead", None, "space")
    aux = P(None, None, None, ("space", "bead"))
    noise = P(None, None, None, None, ("space", "bead"))
    return jax.shard_map(
        on_device, mesh=mesh, in_specs=(wide, wide, wide, P(), P(), aux, noise),
        out_specs=(wide, wide, wide, aux), check_vma=False,
    )
```

```python
import math

import jax
import jax.numpy as jnp
import numpy as np
from jax import lax
from jax.experimental import pallas as pl
from jax.experimental.pallas import tpu as pltpu
from jax.sharding import PartitionSpec as P

BEADS, OWNERS, SPACES, CELL, AUX, STEPS = 32, 32, 4, 128, 4, 2
TIME_STEP, FREQ, LENGTH, STRENGTH = 0.5, 1.5, 2.0, 0.1
HALF = 0.5 * TIME_STEP
SCALE = math.sqrt(math.log2(math.e))
SHIFT = LENGTH * SCALE
F32, BF16 = jnp.float32, jnp.bfloat16
MESH = pl.DeviceIdType.MESH
HIGHEST = lax.Precision.HIGHEST
AHEAD = 1
STAGES = ((0,), (1, 3, 2))
CHUNKS = 1
PART = BEADS // CHUNKS
ORDER1, ORDER2 = (2, 1, 3, 0), (2, 1, 3, 0)


def constants():
    j = np.arange(BEADS, dtype=np.float64)
    phase = 2.0 * np.pi * j[:, None] * j[None, :] / BEADS
    k = j[None, :]
    basis = np.where(k < BEADS // 2, np.sqrt(2.0 / BEADS) * np.cos(phase), np.sqrt(2.0 / BEADS) * np.sin(phase))
    basis = np.where(k == 0, np.sqrt(1.0 / BEADS), basis)
    basis = np.where(k == BEADS // 2, np.sqrt(1.0 / BEADS) * np.cos(np.pi * j[:, None]), basis)
    freq = 2.0 * FREQ * np.sin(np.pi * j / BEADS)
    safe = np.where(j == 0, 1.0, freq)
    sinc = np.where(j == 0, TIME_STEP, np.sin(TIME_STEP * freq) / safe)
    out = np.zeros((5, BEADS, CELL), np.float32)
    out[0, :, :BEADS] = basis.T
    out[1, :, :BEADS] = basis
    out[2] = np.cos(TIME_STEP * freq)[:, None]
    out[3] = sinc[:, None]
    out[4] = (freq * np.sin(TIME_STEP * freq))[:, None]
    return out


def split3(x):
    a = x.astype(BF16).astype(F32)
    r = x - a
    b = r.astype(BF16).astype(F32)
    return a, b, r - b


NN = (((1,), (0,)), ((), ()))


def exponents(xs, yss):
    none = jnp.zeros((48, CELL), BF16)
    sides = []
    for x in xs:
        a, b, c = split3(x)
        sides.append(jnp.concatenate([a, a, b, b, a, c], axis=0).astype(BF16))
    right = jnp.concatenate(
        [jnp.concatenate([sides[0], none], axis=1), jnp.concatenate([none, sides[1]], axis=1)], axis=0
    )
    rows, left = [], []
    for k in range(len(yss[0])):
        parts = [split3(ys[k]) for ys in yss]
        rows.append(jnp.concatenate([v for a, b, c in parts for v in (a, b, a, b, c, a)], axis=0).T.astype(BF16))
        left += [jnp.concatenate([v for a, b, _ in parts for v in (a, b)], axis=0).astype(BF16)] * 2
    e = lax.dot_general(jnp.concatenate(rows, axis=0), right, NN, preferred_element_type=F32)
    return e, jnp.concatenate(left, axis=1)


def pulls(e, left):
    parts = []
    for k in range(e.shape[0] // CELL):
        w = jnp.exp2(e[k * CELL : (k + 1) * CELL])
        hi = w.astype(BF16)
        parts += [hi, (w - hi.astype(F32)).astype(BF16)]
    o = lax.dot_general(left, jnp.concatenate(parts, axis=0), NN, preferred_element_type=F32)
    own = [o[16 * k : 16 * k + 16, CELL * k : CELL * k + CELL] for k in range(2)]
    return [v[:8] + v[8:] for v in own]


def pipelined(cells, x_of, ys_of, done):
    cells, todo = list(cells), []
    pairs = [cells[i : i + 2] for i in range(0, len(cells), 2)]
    for i in range(len(pairs) + AHEAD):
        if i < len(pairs):
            todo.append(exponents([x_of(c) for c in pairs[i]], [ys_of(c) for c in pairs[i]]))
        if i >= AHEAD:
            for c, v in zip(pairs[i - AHEAD], pulls(*todo[i - AHEAD])):
                done(c, v)


def put_fixed(px, others):
    one, zero = jnp.ones((65, CELL), F32), jnp.zeros((65, CELL), F32)
    for ref, row in [(px, 4)] + [(r, 3) for r in others]:
        for r in (row, 5, 6, 7):
            ref[pl.ds(r, 65, stride=8), :] = one if r == row else zero


def put_points(ref, base, tiles, shift, center):
    n = tiles[0].shape[0]
    t = [tiles[0] + shift, tiles[1], tiles[2]] if shift else list(tiles)
    norm = -0.5 * (t[0] * t[0] + t[1] * t[1] + t[2] * t[2])
    for r, v in enumerate(t):
        ref[pl.ds(base + r, n, stride=8), :] = v
    ref[pl.ds(base + (3 if center else 4), n, stride=8), :] = norm


def at(c):
    return pl.ds(pl.multiple_of(c * 8, 8), 8)


def force_of(x, s):
    return (STRENGTH / SCALE) * (x * s[3:4] - s)


def own_cells(px, p0, fb):
    def done(c, v):
        fb[at(c), :] = v

    pipelined(range(64), lambda c: px[at(c), :], lambda c: [p0[at(c), :]], done)


def next_cells(cells, px, pm, pp, fb):
    def done(c, v):
        fb[at(c), :] = force_of(px[at(c), :], fb[at(c), :] + v)

    pipelined(cells, lambda c: px[at(c), :], lambda c: [pm[at(c), :], pp[at(c), :]], done)


def three_cells(cells, px, pm, p0, pp, fb):
    def done(c, v):
        fb[at(c), :] = force_of(px[at(c), :], v)

    pipelined(cells, lambda c: px[at(c), :], lambda c: [pm[at(c), :], p0[at(c), :], pp[at(c + 1), :]], done)


TILES = [(c, h) for c in range(3) for h in range(2)]


def mm(a, b):
    return jnp.dot(a, b, precision=HIGHEST, preferred_element_type=F32)


def take(sem, like, rows):
    part = like.at[pl.ds(0, rows)]
    pltpu.make_async_copy(part, part, sem).wait()


def exchange(me, send, recv, ssem, rsem, first, rows, order, planes=None):
    plane, place = me // 8, lax.rem(me, 8)
    for step in order:
        base = lax.rem(plane + step, 4) * 8
        for k in range(0 if step else 1, 8):
            peer = base + lax.rem(place + k, 8)
            pltpu.make_async_remote_copy(
                src_ref=send.at[pl.ds(pl.multiple_of(peer * 16 + first, 8), rows)],
                dst_ref=recv.at[pl.ds(pl.multiple_of(me * 16 + first, 8), rows)],
                send_sem=ssem,
                recv_sem=rsem if planes is None else planes.at[plane],
                device_id={"bead": peer},
                device_id_type=MESH,
            ).start()
    own = pl.ds(pl.multiple_of(me * 16 + first, 8), 8 * (1 + rows // 8))
    recv[own, :] = send[own, :]
    total = (OWNERS - 1) * rows
    return (lambda: take(rsem, recv, total)), (lambda: take(ssem, send, total))


def body(
    q_hbm, p_hbm, f_hbm, dr_hbm, mx_hbm, aux_hbm, noise_hbm, cst_hbm,
    q_out, p_out, f_out, aux_out,
    q, p, f, dr, mx, aux, noise, cst,
    send, recv, send2, recv2, edge, coef, u, u2, hs, hr,
    px, pm, p0, pp, fb,
    lsem, ssem, rsem, psem, hssem, hrsem, essem, ersem,
):
    s, me = lax.axis_index("space"), lax.axis_index("bead")
    loads = [
        pltpu.make_async_copy(a, b, lsem.at[i])
        for i, (a, b) in enumerate(
            [(q_hbm, q), (p_hbm, p), (f_hbm, f), (dr_hbm, dr), (mx_hbm, mx), (aux_hbm, aux), (noise_hbm, noise), (cst_hbm, cst)]
        )
    ]
    barrier = pltpu.get_barrier_semaphore()
    up, down = lax.rem(s + 1, SPACES), lax.rem(s + SPACES - 1, SPACES)

    plane, place = me // 8, lax.rem(me, 8)
    for step in ORDER1:
        for k in range(0 if step else 1, 8):
            peer = lax.rem(plane + step, 4) * 8 + lax.rem(place + k, 8)
            pl.semaphore_signal(barrier, inc=1, device_id={"bead": peer}, device_id_type=MESH)
    first, last = me == 0, me == OWNERS - 1

    @pl.when(jnp.logical_or(first, last))
    def _():
        there, bead = jnp.where(first, down, up), OWNERS - 1 - me
        pl.semaphore_signal(barrier, inc=1, device_id={"space": there, "bead": bead}, device_id_type=MESH)

    for c in loads:
        c.start()
    for c in loads[:3]:
        c.wait()
    for h in range(2):
        for c in range(3):
            rows = pl.ds(h * 32, 32)
            send[pl.ds(h * 3 + c, 32, stride=16), :] = q[c, rows, :]
            send[pl.ds(6 + h * 3 + c, 32, stride=16), :] = p[c, rows, :] + HALF * f[c, rows, :]
    put_fixed(px, (pm, p0, pp))
    pl.semaphore_wait(barrier, OWNERS - 1 + jnp.where(jnp.logical_or(first, last), 1, 0))
    arrived, sent = exchange(me, send, recv, ssem.at[0], rsem.at[0], 0, 12, ORDER1)

    for c in loads[3:]:
        c.wait()
    for m, ref in enumerate((dr, mx)):
        for a in range(5):
            cols = ref[a].T
            for b in range(5):
                coef[m, a, b] = jnp.broadcast_to(cols[:, b : b + 1], (BEADS, CELL))
    for t, (c, h) in enumerate(TILES):
        lanes = pl.ds(t * CELL, CELL)
        state = [aux[pl.ds(c * 8 + h * 4 + a, 32, stride=24), :] for a in range(AUX)]
        kick = [[noise[st, b, c, :, pl.ds(h * CELL, CELL)] for b in range(5)] for st in range(STEPS)]
        for a in range(5):
            total = coef[1, a, 0] * kick[0][0]
            later = coef[1, a, 0] * kick[1][0]
            for b in range(1, 5):
                total = total + coef[1, a, b] * kick[0][b]
                later = later + coef[1, a, b] * kick[1][b]
            for b in range(AUX):
                total = total + coef[0, a, b + 1] * state[b]
            u[a, :, lanes] = total
            u2[a, :, lanes] = later

    arrived()
    fwd, inv = cst[0][:, :BEADS], cst[1][:, :BEADS]
    wide = lambda v: jnp.concatenate([v] * 6, axis=1)
    cosine, sinc, wsin = wide(cst[2]), wide(cst[3]), wide(cst[4])
    drift0 = [wide(coef[0, a, 0]) for a in range(5)]

    def free(qm, pm_, kick):
        z = drift0[0] * pm_ + kick[0]
        rest = [drift0[a] * pm_ + kick[a] for a in range(1, 5)]
        return qm * cosine + sinc * z, z * cosine - wsin * qm, rest

    qm = mm(fwd, jnp.concatenate([recv[pl.ds(h * 3 + c, 32, stride=16), :] for c, h in TILES], axis=1))
    pmode = mm(fwd, jnp.concatenate([recv[pl.ds(6 + h * 3 + c, 32, stride=16), :] for c, h in TILES], axis=1))
    qm, pmode, state = free(qm, pmode, u)
    points = mm(inv, qm) * SCALE
    tile = lambda v, c, h: v[:, (2 * c + h) * CELL : (2 * c + h + 1) * CELL]
    for h in range(2):
        for c in range(3):
            hs[h, c] = tile(points, c, h)

    halo = []
    for k in range(CHUNKS):
        beads = pl.ds(k * PART, PART)
        for h in range(2):
            mine = s * 64 + h * 32 + me
            for side, step in ((0, 1), (1, 255)):
                there = lax.rem(mine + step, 256)
                slot = lax.rem(there // 32, 2)
                halo.append(
                    pltpu.make_async_remote_copy(
                        src_ref=hs.at[h, :, beads],
                        dst_ref=hr.at[side, slot, :, beads],
                        send_sem=hssem.at[k, side, h],
                        recv_sem=hrsem.at[k, side, slot],
                        device_id={"space": there // 64, "bead": lax.rem(there, 32)},
                        device_id_type=MESH,
                    )
                )
    for c in halo:
        c.start()
    for h in range(2):
        mine = [tile(points, c, h) for c in range(3)]
        put_points(px, h * 256, mine, 0.0, True)
        put_points(p0, h * 256, mine, 0.0, False)
    for a in range(5):
        total = u2[a]
        for b in range(AUX):
            total = total + wide(coef[0, a, b + 1]) * state[b]
        u2[a] = total
    own_cells(px, p0, fb)
    for k in range(CHUNKS):
        beads = pl.ds(k * PART, PART)
        for side, (ref, shift) in enumerate(((pm, -SHIFT), (pp, SHIFT))):
            for h in range(2):
                pltpu.make_async_remote_copy(
                    src_ref=hs.at[h, :, beads], dst_ref=hr.at[side, h, :, beads],
                    send_sem=hssem.at[k, side, h], recv_sem=hrsem.at[k, side, h],
                    device_id={"space": up}, device_id_type=MESH,
                ).wait_recv()
                put_points(ref, h * 256 + k * PART * 8, [hr[side, h, c, beads, :] for c in range(3)], shift, False)
        next_cells([h * 32 + k * PART + i for h in range(2) for i in range(PART)], px, pm, pp, fb)
    force = jnp.concatenate([fb[pl.ds(h * 256 + c, 32, stride=8), :] for c, h in TILES], axis=1)
    pmode = pmode + 2.0 * HALF * mm(fwd, force)
    qm, pmode, state = free(qm, pmode, u2)
    qb = mm(inv, qm)
    for c, h in TILES:
        send2[pl.ds(h * 3 + c, 32, stride=16), :] = tile(qb, c, h)
    _, sent2 = exchange(me, send2, recv2, ssem.at[1], rsem.at[1], 0, 6, ORDER2, psem)

    def edge_copy(side, bead):
        return pltpu.make_async_remote_copy(
            src_ref=send2.at[pl.ds(pl.multiple_of(bead * 16, 16), 6)],
            dst_ref=edge.at[pl.ds(side * 8, 6)],
            send_sem=essem.at[0],
            recv_sem=ersem.at[side],
            device_id={"space": (up, down)[side], "bead": bead},
            device_id_type=MESH,
        )

    def edge_owners(act):
        for side, owner in ((0, last), (1, first)):

            @pl.when(owner)
            def _():
                def one(k, carry):
                    act(edge_copy(side, lax.rem(me + k, OWNERS)))
                    return carry

                lax.fori_loop(0, OWNERS, one, 0)

    edge_owners(lambda copy: copy.start())
    pb = mm(inv, pmode)
    for c, h in TILES:
        send2[pl.ds(8 + h * 3 + c, 32, stride=16), :] = tile(pb, c, h)
    arrived3, sent3 = exchange(me, send2, recv2, ssem.at[2], rsem.at[2], 8, 6, ORDER2)
    for c, h in TILES:
        for a in range(AUX):
            aux_out[pl.ds(c * 8 + h * 4 + a, 32, stride=24), :] = tile(state[a], c, h)
    for c in halo:
        c.wait_send()
    sent()
    for steps in STAGES:
        inner = []
        for step in steps:
            here = lax.rem(plane + step, 4)
            take(psem.at[here], recv2, (8 if step else 7) * 6)
            for h in range(2):
                tiles = [recv2[pl.ds(here * 128 + h * 3 + c, 8, stride=16), :] * SCALE for c in range(3)]
                base = h * 256 + here * 64
                put_points(px, base, tiles, 0.0, True)
                put_points(p0, base, tiles, 0.0, False)
                put_points(pm, base + 8, tiles, -SHIFT, False)
                put_points(pp, base, tiles, SHIFT, False)
            inner += [h * 32 + here * 8 + i for h in range(2) for i in range(1, 7)]
        if steps is STAGES[-1]:
            inner += [8 * i + j for i in range(8) for j in (0, 7)][1:-1]
        three_cells(inner, px, pm, p0, pp, fb)
    for side in range(2):
        edge_copy(side, 0).wait_recv()
    put_points(pm, 0, [edge[3 + c : 4 + c, :] * SCALE for c in range(3)], -SHIFT, False)
    put_points(pp, 512, [edge[8 + c : 9 + c, :] * SCALE for c in range(3)], SHIFT, False)
    three_cells((0, 63), px, pm, p0, pp, fb)
    arrived3()
    for h in range(2):
        rows = pl.ds(h * 32, 32)
        for c in range(3):
            force = fb[pl.ds(h * 256 + c, 32, stride=8), :]
            f_out[c, rows, :] = force
            q_out[c, rows, :] = recv2[pl.ds(h * 3 + c, 32, stride=16), :]
            p_out[c, rows, :] = recv2[pl.ds(8 + h * 3 + c, 32, stride=16), :] + HALF * force
    for owner in (last, first):

        @pl.when(owner)
        def _():
            take(essem.at[0], send2, OWNERS * 6)

    sent2()
    sent3()


def hand_over(*refs):
    copies = [pltpu.make_async_copy(refs[i], refs[4 + i], refs[8].at[i]) for i in range(4)]
    for c in copies:
        c.start()
    for c in copies:
        c.wait()


def on_device(positions, momenta, forces, gle_drift, gle_noise_mix, aux_momenta, noise):
    cells = lambda v: v.reshape(3, 64, CELL)
    modes_last = lambda v: jnp.transpose(v, (1, 2, 0))
    aux = jnp.transpose(aux_momenta.reshape(BEADS, AUX, 3, 2, CELL), (0, 2, 3, 1, 4)).reshape(768, CELL)
    kicks = jnp.transpose(noise, (0, 2, 3, 1, 4))
    big = jax.ShapeDtypeStruct((3, 64, CELL), F32)
    vm = lambda *shape: pltpu.VMEM(shape, F32)
    dma = lambda *shape: pltpu.SemaphoreType.DMA(shape)
    any_, vmem = pl.BlockSpec(memory_space=pl.ANY), pl.BlockSpec(memory_space=pltpu.VMEM)
    shapes = ((3, 64, CELL),) * 3 + ((768, CELL),)
    results = pl.pallas_call(
        body,
        out_shape=tuple(pltpu.VMEM(x, F32) for x in shapes),
        in_specs=[any_] * 8,
        out_specs=(vmem,) * 4,
        scratch_shapes=[
            vm(3, 64, CELL), vm(3, 64, CELL), vm(3, 64, CELL), vm(5, 5, BEADS), vm(5, 5, BEADS),
            vm(768, CELL), vm(2, 5, 3, BEADS, 256), vm(5, BEADS, CELL),
            vm(512, CELL), vm(512, CELL), vm(512, CELL), vm(512, CELL), vm(16, CELL),
            vm(2, 5, 5, BEADS, CELL), vm(5, BEADS, 768), vm(5, BEADS, 768),
            vm(2, 3, BEADS, CELL), vm(2, 2, 3, BEADS, CELL),
            *([vm(520, CELL)] * 5),
            dma(8), dma(3), dma(3), dma(4), dma(CHUNKS, 2, 2), dma(CHUNKS, 2, 2), dma(1), dma(2),
        ],
        compiler_params=pltpu.CompilerParams(collective_id=0, has_side_effects=True),
    )(cells(positions), cells(momenta), cells(forces), modes_last(gle_drift), modes_last(gle_noise_mix), aux, kicks, jnp.asarray(constants()))
    q, p, f, a = pl.pallas_call(
        hand_over,
        out_shape=tuple(jax.ShapeDtypeStruct(x, F32) for x in shapes),
        in_specs=[any_] * 4,
        out_specs=(any_,) * 4,
        scratch_shapes=[dma(4)],
    )(*[pltpu.with_memory_space_constraint(x, pltpu.VMEM) for x in results])
    aux_new = jnp.transpose(a.reshape(BEADS, 3, 2, AUX, CELL), (0, 3, 1, 2, 4)).reshape(BEADS, AUX, 3, 256)
    back = lambda v: v.reshape(1, 3, 8192)
    return back(q), back(p), back(f), aux_new


def solution(mesh):
    wide = P("bead", None, "space")
    aux = P(None, None, None, ("space", "bead"))
    noise = P(None, None, None, None, ("space", "bead"))
    return jax.shard_map(
        on_device, mesh=mesh, in_specs=(wide, wide, wide, P(), P(), aux, noise),
        out_specs=(wide, wide, wide, aux), check_vma=False,
    )
```

```python
import math

import jax
import jax.numpy as jnp
import numpy as np
from jax import lax
from jax.experimental import pallas as pl
from jax.experimental.pallas import tpu as pltpu
from jax.sharding import PartitionSpec as P

BEADS, OWNERS, SPACES, CELL, AUX, STEPS = 32, 32, 4, 128, 4, 2
TIME_STEP, FREQ, LENGTH, STRENGTH = 0.5, 1.5, 2.0, 0.1
HALF = 0.5 * TIME_STEP
SCALE = math.sqrt(math.log2(math.e))
SHIFT = LENGTH * SCALE
F32, BF16 = jnp.float32, jnp.bfloat16
MESH = pl.DeviceIdType.MESH
HIGHEST = lax.Precision.HIGHEST
AHEAD = 1
STAGES = ((0,), (1, 3, 2))
CHUNKS = 1
PART = BEADS // CHUNKS
ORDER1, ORDER2 = (2, 1, 3, 0), (2, 1, 3, 0)


def constants():
    j = np.arange(BEADS, dtype=np.float64)
    phase = 2.0 * np.pi * j[:, None] * j[None, :] / BEADS
    k = j[None, :]
    basis = np.where(k < BEADS // 2, np.sqrt(2.0 / BEADS) * np.cos(phase), np.sqrt(2.0 / BEADS) * np.sin(phase))
    basis = np.where(k == 0, np.sqrt(1.0 / BEADS), basis)
    basis = np.where(k == BEADS // 2, np.sqrt(1.0 / BEADS) * np.cos(np.pi * j[:, None]), basis)
    freq = 2.0 * FREQ * np.sin(np.pi * j / BEADS)
    safe = np.where(j == 0, 1.0, freq)
    sinc = np.where(j == 0, TIME_STEP, np.sin(TIME_STEP * freq) / safe)
    out = np.zeros((5, BEADS, CELL), np.float32)
    out[0, :, :BEADS] = basis.T
    out[1, :, :BEADS] = basis
    out[2] = np.cos(TIME_STEP * freq)[:, None]
    out[3] = sinc[:, None]
    out[4] = (freq * np.sin(TIME_STEP * freq))[:, None]
    return out


def split3(x):
    a = x.astype(BF16).astype(F32)
    r = x - a
    b = r.astype(BF16).astype(F32)
    return a, b, r - b


NN = (((1,), (0,)), ((), ()))


def exponents(xs, yss):
    none = jnp.zeros((48, CELL), BF16)
    sides = []
    for x in xs:
        a, b, c = split3(x)
        sides.append(jnp.concatenate([a, a, b, b, a, c], axis=0).astype(BF16))
    right = jnp.concatenate(
        [jnp.concatenate([sides[0], none], axis=1), jnp.concatenate([none, sides[1]], axis=1)], axis=0
    )
    rows, left = [], []
    for k in range(len(yss[0])):
        parts = [split3(ys[k]) for ys in yss]
        rows.append(jnp.concatenate([v for a, b, c in parts for v in (a, b, a, b, c, a)], axis=0).T.astype(BF16))
        left += [jnp.concatenate([v for a, b, _ in parts for v in (a, b)], axis=0).astype(BF16)] * 2
    e = lax.dot_general(jnp.concatenate(rows, axis=0), right, NN, preferred_element_type=F32)
    return e, jnp.concatenate(left, axis=1)


def pulls(e, left):
    parts = []
    for k in range(e.shape[0] // CELL):
        w = jnp.exp2(e[k * CELL : (k + 1) * CELL])
        hi = w.astype(BF16)
        parts += [hi, (w - hi.astype(F32)).astype(BF16)]
    o = lax.dot_general(left, jnp.concatenate(parts, axis=0), NN, preferred_element_type=F32)
    own = [o[16 * k : 16 * k + 16, CELL * k : CELL * k + CELL] for k in range(2)]
    return [v[:8] + v[8:] for v in own]


def pipelined(cells, x_of, ys_of, done):
    cells, todo = list(cells), []
    pairs = [cells[i : i + 2] for i in range(0, len(cells), 2)]
    for i in range(len(pairs) + AHEAD):
        if i < len(pairs):
            todo.append(exponents([x_of(c) for c in pairs[i]], [ys_of(c) for c in pairs[i]]))
        if i >= AHEAD:
            for c, v in zip(pairs[i - AHEAD], pulls(*todo[i - AHEAD])):
                done(c, v)


def put_fixed(px, others):
    one, zero = jnp.ones((65, CELL), F32), jnp.zeros((65, CELL), F32)
    for ref, row in [(px, 4)] + [(r, 3) for r in others]:
        for r in (row, 5, 6, 7):
            ref[pl.ds(r, 65, stride=8), :] = one if r == row else zero


def put_points(ref, base, tiles, shift, center):
    n = tiles[0].shape[0]
    t = [tiles[0] + shift, tiles[1], tiles[2]] if shift else list(tiles)
    norm = -0.5 * (t[0] * t[0] + t[1] * t[1] + t[2] * t[2])
    for r, v in enumerate(t):
        ref[pl.ds(base + r, n, stride=8), :] = v
    ref[pl.ds(base + (3 if center else 4), n, stride=8), :] = norm


def at(c):
    return pl.ds(pl.multiple_of(c * 8, 8), 8)


def force_of(x, s):
    return (STRENGTH / SCALE) * (x * s[3:4] - s)


def own_cells(px, p0, fb):
    def done(c, v):
        fb[at(c), :] = v

    pipelined(range(64), lambda c: px[at(c), :], lambda c: [p0[at(c), :]], done)


def next_cells(cells, px, pm, pp, fb):
    def done(c, v):
        fb[at(c), :] = force_of(px[at(c), :], fb[at(c), :] + v)

    pipelined(cells, lambda c: px[at(c), :], lambda c: [pm[at(c), :], pp[at(c), :]], done)


def three_cells(cells, px, pm, p0, pp, fb):
    def done(c, v):
        fb[at(c), :] = force_of(px[at(c), :], v)

    pipelined(cells, lambda c: px[at(c), :], lambda c: [pm[at(c), :], p0[at(c), :], pp[at(c + 1), :]], done)


TILES = [(c, h) for c in range(3) for h in range(2)]


def mm(a, b):
    return jnp.dot(a, b, precision=HIGHEST, preferred_element_type=F32)


def take(sem, like, rows):
    part = like.at[pl.ds(0, rows)]
    pltpu.make_async_copy(part, part, sem).wait()


def exchange(me, send, recv, ssem, rsem, first, rows, order, planes=None):
    plane, place = me // 8, lax.rem(me, 8)
    for step in order:
        base = lax.rem(plane + step, 4) * 8
        for k in range(0 if step else 1, 8):
            peer = base + lax.rem(place + k, 8)
            pltpu.make_async_remote_copy(
                src_ref=send.at[pl.ds(pl.multiple_of(peer * 16 + first, 8), rows)],
                dst_ref=recv.at[pl.ds(pl.multiple_of(me * 16 + first, 8), rows)],
                send_sem=ssem,
                recv_sem=rsem if planes is None else planes.at[plane],
                device_id={"bead": peer},
                device_id_type=MESH,
            ).start()
    own = pl.ds(pl.multiple_of(me * 16 + first, 8), 8 * (1 + rows // 8))
    recv[own, :] = send[own, :]
    total = (OWNERS - 1) * rows
    return (lambda: take(rsem, recv, total)), (lambda: take(ssem, send, total))


def body(
    q_hbm, p_hbm, f_hbm, dr_hbm, mx_hbm, aux_hbm, noise_hbm, cst_hbm,
    q_out, p_out, f_out, aux_out,
    q, p, f, dr, mx, aux, noise, cst,
    send, recv, send2, recv2, edge, coef, u, u2, hs, hr,
    px, pm, p0, pp, fb,
    lsem, ssem, rsem, psem, hssem, hrsem, essem, ersem,
):
    s, me = lax.axis_index("space"), lax.axis_index("bead")
    loads = [
        pltpu.make_async_copy(a, b, lsem.at[i])
        for i, (a, b) in enumerate(
            [(q_hbm, q), (p_hbm, p), (f_hbm, f), (dr_hbm, dr), (mx_hbm, mx), (aux_hbm, aux), (noise_hbm, noise), (cst_hbm, cst)]
        )
    ]
    barrier = pltpu.get_barrier_semaphore()
    up, down = lax.rem(s + 1, SPACES), lax.rem(s + SPACES - 1, SPACES)

    plane, place = me // 8, lax.rem(me, 8)
    for step in ORDER1:
        for k in range(0 if step else 1, 8):
            peer = lax.rem(plane + step, 4) * 8 + lax.rem(place + k, 8)
            pl.semaphore_signal(barrier, inc=1, device_id={"bead": peer}, device_id_type=MESH)
    first, last = me == 0, me == OWNERS - 1

    @pl.when(jnp.logical_or(first, last))
    def _():
        there, bead = jnp.where(first, down, up), OWNERS - 1 - me
        pl.semaphore_signal(barrier, inc=1, device_id={"space": there, "bead": bead}, device_id_type=MESH)

    for c in loads:
        c.start()
    for c in loads[:3]:
        c.wait()
    for h in range(2):
        for c in range(3):
            rows = pl.ds(h * 32, 32)
            send[pl.ds(h * 3 + c, 32, stride=16), :] = q[c, rows, :]
            send[pl.ds(6 + h * 3 + c, 32, stride=16), :] = p[c, rows, :] + HALF * f[c, rows, :]
    put_fixed(px, (pm, p0, pp))
    pl.semaphore_wait(barrier, OWNERS - 1 + jnp.where(jnp.logical_or(first, last), 1, 0))
    arrived, sent = exchange(me, send, recv, ssem.at[0], rsem.at[0], 0, 12, ORDER1)

    for c in loads[3:]:
        c.wait()
    for m, ref in enumerate((dr, mx)):
        for a in range(5):
            cols = ref[a].T
            for b in range(5):
                coef[m, a, b] = jnp.broadcast_to(cols[:, b : b + 1], (BEADS, CELL))
    for t, (c, h) in enumerate(TILES):
        lanes = pl.ds(t * CELL, CELL)
        state = [aux[pl.ds(c * 8 + h * 4 + a, 32, stride=24), :] for a in range(AUX)]
        kick = [[noise[st, b, c, :, pl.ds(h * CELL, CELL)] for b in range(5)] for st in range(STEPS)]
        for a in range(5):
            total = coef[1, a, 0] * kick[0][0]
            later = coef[1, a, 0] * kick[1][0]
            for b in range(1, 5):
                total = total + coef[1, a, b] * kick[0][b]
                later = later + coef[1, a, b] * kick[1][b]
            for b in range(AUX):
                total = total + coef[0, a, b + 1] * state[b]
            u[a, :, lanes] = total
            u2[a, :, lanes] = later

    arrived()
    fwd, inv = cst[0][:, :BEADS], cst[1][:, :BEADS]
    wide = lambda v: jnp.concatenate([v] * 6, axis=1)
    cosine, sinc, wsin = wide(cst[2]), wide(cst[3]), wide(cst[4])
    drift0 = [wide(coef[0, a, 0]) for a in range(5)]

    def free(qm, pm_, kick):
        z = drift0[0] * pm_ + kick[0]
        rest = [drift0[a] * pm_ + kick[a] for a in range(1, 5)]
        return qm * cosine + sinc * z, z * cosine - wsin * qm, rest

    qm = mm(fwd, jnp.concatenate([recv[pl.ds(h * 3 + c, 32, stride=16), :] for c, h in TILES], axis=1))
    pmode = mm(fwd, jnp.concatenate([recv[pl.ds(6 + h * 3 + c, 32, stride=16), :] for c, h in TILES], axis=1))
    qm, pmode, state = free(qm, pmode, u)
    points = mm(inv, qm) * SCALE
    tile = lambda v, c, h: v[:, (2 * c + h) * CELL : (2 * c + h + 1) * CELL]
    for h in range(2):
        for c in range(3):
            hs[h, c] = tile(points, c, h)

    halo = []
    for k in range(CHUNKS):
        beads = pl.ds(k * PART, PART)
        for h in range(2):
            mine = s * 64 + h * 32 + me
            for side, step in ((0, 1), (1, 255)):
                there = lax.rem(mine + step, 256)
                slot = lax.rem(there // 32, 2)
                halo.append(
                    pltpu.make_async_remote_copy(
                        src_ref=hs.at[h, :, beads],
                        dst_ref=hr.at[side, slot, :, beads],
                        send_sem=hssem.at[k, side, h],
                        recv_sem=hrsem.at[k, side, slot],
                        device_id={"space": there // 64, "bead": lax.rem(there, 32)},
                        device_id_type=MESH,
                    )
                )
    for c in halo:
        c.start()
    for h in range(2):
        mine = [tile(points, c, h) for c in range(3)]
        put_points(px, h * 256, mine, 0.0, True)
        put_points(p0, h * 256, mine, 0.0, False)
    for a in range(5):
        total = u2[a]
        for b in range(AUX):
            total = total + wide(coef[0, a, b + 1]) * state[b]
        u2[a] = total
    own_cells(px, p0, fb)
    for k in range(CHUNKS):
        beads = pl.ds(k * PART, PART)
        for side, (ref, shift) in enumerate(((pm, -SHIFT), (pp, SHIFT))):
            for h in range(2):
                pltpu.make_async_remote_copy(
                    src_ref=hs.at[h, :, beads], dst_ref=hr.at[side, h, :, beads],
                    send_sem=hssem.at[k, side, h], recv_sem=hrsem.at[k, side, h],
                    device_id={"space": up}, device_id_type=MESH,
                ).wait_recv()
                put_points(ref, h * 256 + k * PART * 8, [hr[side, h, c, beads, :] for c in range(3)], shift, False)
        next_cells([h * 32 + k * PART + i for h in range(2) for i in range(PART)], px, pm, pp, fb)
    force = jnp.concatenate([fb[pl.ds(h * 256 + c, 32, stride=8), :] for c, h in TILES], axis=1)
    pmode = pmode + 2.0 * HALF * mm(fwd, force)
    qm, pmode, state = free(qm, pmode, u2)
    qb = mm(inv, qm)
    for c, h in TILES:
        send2[pl.ds(h * 3 + c, 32, stride=16), :] = tile(qb, c, h)
    _, sent2 = exchange(me, send2, recv2, ssem.at[1], rsem.at[1], 0, 6, ORDER2, psem)

    def edge_copy(side, bead):
        return pltpu.make_async_remote_copy(
            src_ref=send2.at[pl.ds(pl.multiple_of(bead * 16, 16), 6)],
            dst_ref=edge.at[pl.ds(side * 8, 6)],
            send_sem=essem.at[0],
            recv_sem=ersem.at[side],
            device_id={"space": (up, down)[side], "bead": bead},
            device_id_type=MESH,
        )

    def edge_owners(act):
        for side, owner in ((0, last), (1, first)):

            @pl.when(owner)
            def _():
                def one(k, carry):
                    act(edge_copy(side, lax.rem(me + k, OWNERS)))
                    return carry

                lax.fori_loop(0, OWNERS, one, 0)

    edge_owners(lambda copy: copy.start())
    pb = mm(inv, pmode)
    for c, h in TILES:
        send2[pl.ds(8 + h * 3 + c, 32, stride=16), :] = tile(pb, c, h)
    arrived3, sent3 = exchange(me, send2, recv2, ssem.at[2], rsem.at[2], 8, 6, ORDER2)
    for c, h in TILES:
        for a in range(AUX):
            aux_out[pl.ds(c * 8 + h * 4 + a, 32, stride=24), :] = tile(state[a], c, h)
    for c in halo:
        c.wait_send()
    sent()
    for steps in STAGES:
        inner = []
        for step in steps:
            here = lax.rem(plane + step, 4)
            take(psem.at[here], recv2, (8 if step else 7) * 6)
            for h in range(2):
                tiles = [recv2[pl.ds(here * 128 + h * 3 + c, 8, stride=16), :] * SCALE for c in range(3)]
                base = h * 256 + here * 64
                put_points(px, base, tiles, 0.0, True)
                put_points(p0, base, tiles, 0.0, False)
                put_points(pm, base + 8, tiles, -SHIFT, False)
                put_points(pp, base, tiles, SHIFT, False)
            inner += [h * 32 + here * 8 + i for h in range(2) for i in range(1, 7)]
        if steps is STAGES[-1]:
            inner += [8 * i + j for i in range(8) for j in (0, 7)][1:-1]
        three_cells(inner, px, pm, p0, pp, fb)
    for side in range(2):
        edge_copy(side, 0).wait_recv()
    put_points(pm, 0, [edge[3 + c : 4 + c, :] * SCALE for c in range(3)], -SHIFT, False)
    put_points(pp, 512, [edge[8 + c : 9 + c, :] * SCALE for c in range(3)], SHIFT, False)
    three_cells((0, 63), px, pm, p0, pp, fb)
    arrived3()
    for h in range(2):
        rows = pl.ds(h * 32, 32)
        for c in range(3):
            force = fb[pl.ds(h * 256 + c, 32, stride=8), :]
            f_out[c, rows, :] = force
            q_out[c, rows, :] = recv2[pl.ds(h * 3 + c, 32, stride=16), :]
            p_out[c, rows, :] = recv2[pl.ds(8 + h * 3 + c, 32, stride=16), :] + HALF * force
    for owner in (last, first):

        @pl.when(owner)
        def _():
            take(essem.at[0], send2, OWNERS * 6)

    sent2()
    sent3()


def hand_over(*refs):
    copies = [pltpu.make_async_copy(refs[i], refs[4 + i], refs[8].at[i]) for i in range(4)]
    for c in copies:
        c.start()
    for c in copies:
        c.wait()


def on_device(positions, momenta, forces, gle_drift, gle_noise_mix, aux_momenta, noise):
    cells = lambda v: v.reshape(3, 64, CELL)
    modes_last = lambda v: jnp.transpose(v, (1, 2, 0))
    aux = jnp.transpose(aux_momenta.reshape(BEADS, AUX, 3, 2, CELL), (0, 2, 3, 1, 4)).reshape(768, CELL)
    kicks = jnp.transpose(noise, (0, 2, 3, 1, 4))
    big = jax.ShapeDtypeStruct((3, 64, CELL), F32)
    vm = lambda *shape: pltpu.VMEM(shape, F32)
    dma = lambda *shape: pltpu.SemaphoreType.DMA(shape)
    any_, vmem = pl.BlockSpec(memory_space=pl.ANY), pl.BlockSpec(memory_space=pltpu.VMEM)
    shapes = ((3, 64, CELL),) * 3 + ((768, CELL),)
    results = pl.pallas_call(
        body,
        out_shape=tuple(pltpu.VMEM(x, F32) for x in shapes),
        in_specs=[any_] * 8,
        out_specs=(vmem,) * 4,
        scratch_shapes=[
            vm(3, 64, CELL), vm(3, 64, CELL), vm(3, 64, CELL), vm(5, 5, BEADS), vm(5, 5, BEADS),
            vm(768, CELL), vm(2, 5, 3, BEADS, 256), vm(5, BEADS, CELL),
            vm(512, CELL), vm(512, CELL), vm(512, CELL), vm(512, CELL), vm(24, CELL),
            vm(2, 5, 5, BEADS, CELL), vm(5, BEADS, 768), vm(5, BEADS, 768),
            vm(2, 3, BEADS, CELL), vm(2, 2, 3, BEADS, CELL),
            *([vm(576, CELL)] * 5),
            dma(8), dma(3), dma(3), dma(4), dma(CHUNKS, 2, 2), dma(CHUNKS, 2, 2), dma(1), dma(2),
        ],
        compiler_params=pltpu.CompilerParams(collective_id=0, has_side_effects=True),
    )(cells(positions), cells(momenta), cells(forces), modes_last(gle_drift), modes_last(gle_noise_mix), aux, kicks, jnp.asarray(constants()))
    q, p, f, a = pl.pallas_call(
        hand_over,
        out_shape=tuple(jax.ShapeDtypeStruct(x, F32) for x in shapes),
        in_specs=[any_] * 4,
        out_specs=(any_,) * 4,
        scratch_shapes=[dma(4)],
    )(*[pltpu.with_memory_space_constraint(x, pltpu.VMEM) for x in results])
    aux_new = jnp.transpose(a.reshape(BEADS, 3, 2, AUX, CELL), (0, 3, 1, 2, 4)).reshape(BEADS, AUX, 3, 256)
    back = lambda v: v.reshape(1, 3, 8192)
    return back(q), back(p), back(f), aux_new


def solution(mesh):
    wide = P("bead", None, "space")
    aux = P(None, None, None, ("space", "bead"))
    noise = P(None, None, None, None, ("space", "bead"))
    return jax.shard_map(
        on_device, mesh=mesh, in_specs=(wide, wide, wide, P(), P(), aux, noise),
        out_specs=(wide, wide, wide, aux), check_vma=False,
    )
```
